512 devices in a mesh: vocab: 64 (over x, z), rows: 8 (over y, core).
Axes of the slice: x: 4, y: 4, z: 16, core: 2. Of those that a mesh axis runs over, the one named last changes fastest.
Arguments:
- hidden: bfloat16 [4096, 4096], P('rows', 'vocab'), may hold values from -48 to 48
- head_weight: bfloat16 [4096, 65536], P('rows', 'vocab'), may hold values from -1 to 1
- in_proj: bfloat16 [4096, 64], replicated, may hold values from -0.09375 to 0.09375
- out_proj: bfloat16 [65536, 64], P('vocab'), may hold values from -6 to 6
- targets: int32 [4096], P('rows'), may hold values from 0 to 65535
- lengths: int32 [32], replicated, may hold values from 1 to 128, as said below
- grad_store: bfloat16 [131072, 4096], P(('vocab', 'rows')), may hold values from -0.09375 to 0.09375
Outputs:
- scores: float32 [32, 131072], P(None, ('vocab', 'rows'))
The draws below stay inside these ranges and needn't reach their ends.
Inputs may be any that keep to these rules, and one draw needn't show every extreme that they name: `lengths`: at least one sequence has exactly 128 valid rows.
All inputs are finite; a program needn't handle non-finite values.
Results may differ from the reference program's by a relative error of at most 0.0029.
Values may be sent and summed in bfloat16 or wider, within the bound.
No kernel may reach another device: no remote copies, remote signals or barrier semaphores. Data moves between devices by JAX's collectives and lax.ppermute only.
A program may use at most 64 MiB of HBM per device.

```python
import math
import jax
import jax.numpy as jnp
from jax import lax

D = 4096
VOCAB = 65536
K = 64
TILE = 128
TOKENS = 4096
NSEQ = 32
NSTORE = 131072


def head_column(head_key, column):
    values = jax.random.normal(jax.random.fold_in(head_key, column), (D,), jnp.float32)
    return jnp.clip(values, -6.0, 6.0) / math.sqrt(D)


def draw_head_weight(key, part):
    head_key = jax.random.fold_in(key, 11)
    columns = jax.vmap(lambda column: head_column(head_key, column))(jnp.arange(VOCAB, dtype=jnp.int32))
    return columns.T.astype(jnp.bfloat16)


def draw_hidden(key, part):
    base_key = jax.random.fold_in(key, 12)
    values = jnp.clip(jax.random.normal(base_key, (TOKENS, D), jnp.float32), -6.0, 6.0)
    return jnp.clip(values, -48.0, 48.0).astype(jnp.bfloat16)


def draw_lengths(key, part):
    drawn = jax.random.randint(jax.random.fold_in(key, 13), (NSEQ,), 1, TILE + 1)
    longest = jax.random.randint(jax.random.fold_in(key, 14), (), 0, NSEQ)
    return drawn.at[longest].set(TILE).astype(jnp.int32)


def touch_ends(values, own_key, least, largest):
    dims = values.shape
    index_at = [jax.random.randint(jax.random.fold_in(own_key, axis), (), 0, dims[axis]) for axis in range(len(dims))]
    values = values.at[tuple(index_at)].set(least)
    longest = dims.index(max(dims))
    index_at[longest] = (index_at[longest] + 1) % dims[longest]
    return values.at[tuple(index_at)].set(largest)


def steps_of(rng, dims, cuts, least, top_value):
    level, own = 1.0, jax.random.fold_in(rng, 6)
    for axis_at, shards_of in cuts:
        draws = jnp.exp(jax.random.uniform(jax.random.fold_in(own, axis_at), (shards_of,), jnp.float32, least / len(cuts), top_value / len(cuts)))
        level = level * jnp.repeat(draws, dims[axis_at] // shards_of).reshape([-1 if axis == axis_at else 1 for axis in range(len(dims))])
    return level


def scatter_about(key, extent, spread, most, pieces=(), kind=jnp.bfloat16):
    values = jax.random.normal(key, extent, jnp.float32) * spread
    if len(pieces) > 0:
        values = steps_of(key, extent, pieces, -0.22, 0.18) * values
    return jnp.clip(values, min=-most, max=most).astype(kind)


def setup_inputs(seed: int = 0) -> dict:
    key_list = jax.random.split(jax.random.key(seed), 8)
    hidden = draw_hidden(jax.random.fold_in(key_list[7], 71), 0)
    head_weight = draw_head_weight(jax.random.fold_in(key_list[7], 71), 0)
    in_proj = scatter_about(key_list[2], (D, K), D ** -0.5, 0.09375)
    out_proj = scatter_about(key_list[3], (VOCAB, K), 1.0, 6.0, ((0, 64),))
    targets = touch_ends(jax.random.randint(key_list[4], (TOKENS,), 0, VOCAB), jax.random.fold_in(key_list[4], 1), 0, VOCAB - 1).astype(jnp.int32)
    lengths = draw_lengths(jax.random.fold_in(key_list[7], 71), 0)
    grad_store = scatter_about(key_list[6], (NSTORE, K * K), (K * K) ** -0.5, 0.09375, ((0, 512),))
    return {"hidden": hidden, "head_weight": head_weight, "in_proj": in_proj, "out_proj": out_proj, "targets": targets, "lengths": lengths, "grad_store": grad_store}


damping_ratio = 0.1
tiny_value = 1e-06

def whiten(seq_grads, cov_out, cov_in):
    proj_width = cov_out.shape[0]
    seq_count = seq_grads.shape[0]
    identity = jnp.eye(proj_width, dtype=jnp.float32)
    damp_out = damping_ratio * jnp.trace(cov_out) / proj_width + tiny_value
    damp_in = damping_ratio * jnp.trace(cov_in) / proj_width + tiny_value
    lower_out = jnp.linalg.cholesky(cov_out + damp_out * identity)
    lower_in = jnp.linalg.cholesky(cov_in + damp_in * identity)
    stacked = jnp.transpose(seq_grads, (1, 0, 2)).reshape(proj_width, seq_count * proj_width)
    left_half = lax.linalg.triangular_solve(lower_out, stacked, left_side=True, lower=True)
    left_full = lax.linalg.triangular_solve(lower_out, left_half, left_side=True, lower=True, transpose_a=True)
    rows_form = jnp.transpose(left_full.reshape(proj_width, seq_count, proj_width), (1, 0, 2)).reshape(seq_count * proj_width, proj_width)
    right_half = lax.linalg.triangular_solve(lower_in, rows_form, left_side=False, lower=True, transpose_a=True)
    right_full = lax.linalg.triangular_solve(lower_in, right_half, left_side=False, lower=True)
    return right_full.reshape(seq_count, proj_width * proj_width)

def reference(hidden, head_weight, in_proj, out_proj, targets, lengths, grad_store):
    vocab_size = head_weight.shape[1]
    proj_width = in_proj.shape[1]
    seq_count = lengths.shape[0]
    out_table = out_proj.astype(jnp.float32)
    columns = jnp.arange(vocab_size, dtype=jnp.int32)

    def tile_grad(inputs):
        tile_rows, tile_targets = inputs
        logits = jnp.dot(tile_rows.astype(jnp.float32), head_weight.astype(jnp.float32), preferred_element_type=jnp.float32)
        row_max = lax.optimization_barrier(jnp.max(logits, axis=1, keepdims=True))
        exponent = jnp.exp(logits - row_max)
        probability = exponent / lax.optimization_barrier(jnp.sum(exponent, axis=1, keepdims=True))
        onehot = (columns[None, :] == tile_targets[:, None]).astype(jnp.float32)
        return jnp.dot(probability - onehot, out_table, precision=lax.Precision.HIGHEST)
    out_grad = lax.map(tile_grad, (hidden.reshape(seq_count, TILE, -1), targets.reshape(seq_count, TILE)))
    input_proj = jnp.dot(hidden.astype(jnp.float32), in_proj.astype(jnp.float32), preferred_element_type=jnp.float32).reshape(seq_count, TILE, proj_width)
    position = jnp.arange(TILE, dtype=jnp.int32)
    is_valid = (position[None, :] < lengths[:, None]).astype(jnp.float32)[:, :, None]
    out_grad = out_grad * is_valid
    input_proj = input_proj * is_valid
    row_total = jnp.sum(lengths).astype(jnp.float32)
    flat_out = out_grad.reshape(-1, proj_width)
    flat_in = input_proj.reshape(-1, proj_width)
    cov_out = jnp.dot(flat_out.T, flat_out, precision=lax.Precision.HIGHEST) / row_total
    cov_in = jnp.dot(flat_in.T, flat_in, precision=lax.Precision.HIGHEST) / row_total
    seq_grads = jnp.einsum('stk,stj->skj', out_grad, input_proj, precision=lax.Precision.HIGHEST)
    seq_grads = seq_grads / jnp.sqrt(lengths.astype(jnp.float32))[:, None, None]
    whitened = whiten(seq_grads, cov_out, cov_in).astype(jnp.bfloat16)
    return jnp.dot(whitened.astype(jnp.float32), grad_store.T.astype(jnp.float32), preferred_element_type=jnp.float32)
```

```python
import functools
import jax
import jax.numpy as jnp
from jax import lax
from jax.experimental import pallas as pl
from jax.experimental.pallas import tpu as pltpu
from jax.sharding import Mesh, PartitionSpec as P

TILE = 128
NX, NZ, NY, NC = 4, 16, 4, 2

damping_ratio = 0.1
tiny_value = 1e-06
HI = lax.Precision.HIGHEST
F32 = jnp.float32
BF16 = jnp.bfloat16


def shift(value, axis, step, size):
    return lax.ppermute(value, axis, [(i, (i + step) % size) for i in range(size)])


def spread(value, axis, size):
    copies = jnp.broadcast_to(value[None], (size,) + value.shape)
    return lax.all_to_all(copies, axis, 0, 0, tiled=True)


def exchange(value, axis):
    return lax.all_to_all(value, axis, 0, 0, tiled=True)


def logits_kernel(offsets, place_ref, *refs):
    count = len(offsets)
    chunks = refs[:count]
    head, in_proj, out_proj, targets, packed, proj = refs[count : count + 6]
    feat_buf, head_buf, proj_buf, logit_buf, sems = refs[count + 6 :]
    x, z = place_ref[0], place_ref[1]
    width = chunks[0].shape[1]
    group = width // NX
    stride = head.shape[0] // NX
    copies = []
    for j, offset in enumerate(offsets):
        copy = pltpu.make_async_copy(chunks[j], feat_buf.at[:, pl.ds(j * width, width)], sems.at[j])
        copy.start()
        copies.append(copy)
        other = (z + offset + NZ) % NZ
        for i in range(NX):
            first = pl.multiple_of(i * stride + other * group, group)
            copy = pltpu.make_async_copy(
                head.at[pl.ds(first, group), :],
                head_buf.at[pl.ds(j * width + i * group, group), :],
                sems.at[count + j * NX + i],
            )
            copy.start()
            copies.append(copy)
            proj_buf[pl.ds(j * width + i * group, group), :] = in_proj[pl.ds(first, group), :]
    for copy in copies:
        copy.wait()
    cols = head.shape[1]
    block = 256

    def column_block(n, carry):
        first = pl.multiple_of(n * block, block)
        logit_buf[:, pl.ds(first, block)] = jnp.dot(
            feat_buf[...], head_buf[:, pl.ds(first, block)], preferred_element_type=F32
        )
        return carry

    lax.fori_loop(0, cols // block, column_block, 0)
    own = pl.multiple_of(x * TILE, TILE)
    proj[...] = jnp.dot(feat_buf[pl.ds(own, TILE), :], proj_buf[...], preferred_element_type=F32)
    table = out_proj[...]
    vocab_first = (x * NZ + z) * cols

    def row_block(i, carry):
        first = pl.multiple_of(i * TILE, TILE)
        logits = logit_buf[pl.ds(first, TILE), :]
        peak = jnp.max(logits, axis=1, keepdims=True)
        weight = jnp.exp(logits - peak)
        total = jnp.sum(weight, axis=1, keepdims=True)
        part1 = weight.astype(BF16)
        rest = weight - part1.astype(F32)
        part2 = rest.astype(BF16)
        part3 = (rest - part2.astype(F32)).astype(BF16)
        mixed = jnp.dot(part1, table, preferred_element_type=F32)
        mixed += jnp.dot(part2, table, preferred_element_type=F32)
        mixed += jnp.dot(part3, table, preferred_element_type=F32)
        column = lax.broadcasted_iota(jnp.int32, logits.shape, 1) + vocab_first
        hit = jnp.where(column == targets[pl.ds(first, TILE), :], 1.0, 0.0).astype(BF16)
        picked = jnp.dot(hit, table, preferred_element_type=F32)
        packed[i, 0:TILE, :] = jnp.concatenate([mixed, picked], axis=1)
        half = mixed.shape
        packed[i, TILE : 2 * TILE, :] = jnp.concatenate(
            [jnp.broadcast_to(peak, half), jnp.broadcast_to(total, half)], axis=1
        )
        return carry

    lax.fori_loop(0, NX, row_block, 0)


def merge(parts, size):
    width = 64
    peaks = [stat[:, 0:1] for _, stat in parts]
    peak = functools.reduce(jnp.maximum, peaks)
    scales = [jnp.exp(p - peak) for p in peaks]
    total = sum(s * stat[:, width : width + 1] for s, (_, stat) in zip(scales, parts))
    mixed = sum(s * data[:, :width] for s, (data, _) in zip(scales, parts))
    picked = sum(data[:, width:] for data, _ in parts)
    return mixed, picked, peak, total


def merge_x_kernel(packed, out):
    parts = [(packed[i, 0:TILE, :], packed[i, TILE : 2 * TILE, :]) for i in range(NX)]
    mixed, picked, peak, total = merge(parts, NX)
    data = jnp.concatenate([mixed, picked], axis=1)
    stat = jnp.concatenate([jnp.broadcast_to(peak, mixed.shape), jnp.broadcast_to(total, mixed.shape)], axis=1)
    rows = TILE // NZ
    out[:, 0:rows, :] = data.reshape(NZ, rows, TILE)
    out[:, rows : 2 * rows, :] = stat.reshape(NZ, rows, TILE)


def merge_z_kernel(packed, out):
    rows = TILE // NZ
    parts = [(packed[i, 0:rows, :], packed[i, rows : 2 * rows, :]) for i in range(NZ)]
    mixed, picked, peak, total = merge(parts, NZ)
    grad = mixed / total - picked
    out[...] = jnp.concatenate([grad, jnp.zeros_like(grad)], axis=1)


def gram_kernel(place_ref, lengths, grads, proj, out):
    seq = place_ref[2]
    length = lengths[seq]
    both = jnp.concatenate([grads[...].reshape(TILE, TILE)[:, :64], proj[...]], axis=1)
    row = lax.broadcasted_iota(jnp.int32, both.shape, 0)
    both = jnp.where(row < length, both, 0.0)
    gram = lax.dot_general(both, both, (((0,), (0,)), ((), ())), precision=HI, preferred_element_type=F32)
    root = jnp.sqrt(jnp.full((64, 64), length.astype(F32)))
    out[0:64, 0:64] = gram[0:64, 0:64]
    out[0:64, 64:128] = gram[0:64, 64:128] / root
    out[64:96, 0:64] = gram[64:96, 64:128]
    out[64:96, 64:128] = gram[96:128, 64:128]


def inverse_kernel(lengths, grams, out):
    total = functools.reduce(jnp.add, [lengths[s] for s in range(lengths.shape[0])]).astype(F32)
    summed = functools.reduce(jnp.add, [grams[d] for d in range(grams.shape[0])])
    cov_out = summed[0:64, 0:64]
    cov_in = jnp.concatenate([summed[64:96, 0:64], summed[64:96, 64:128]], axis=0)
    work = jnp.concatenate([cov_out, cov_in], axis=1) / total
    row = lax.broadcasted_iota(jnp.int32, work.shape, 0)
    lane = lax.broadcasted_iota(jnp.int32, work.shape, 1)
    left = lane < 64
    inner = jnp.where(left, lane, lane - 64)
    diag = jnp.where(row == inner, work, 0.0)
    trace_out = jnp.sum(jnp.where(left, diag, 0.0))
    trace_in = jnp.sum(jnp.where(left, 0.0, diag))
    damp = jnp.where(left, damping_ratio * trace_out / 64 + tiny_value, damping_ratio * trace_in / 64 + tiny_value)
    work = work + jnp.where(row == inner, damp, 0.0)

    def step(k, work):
        at_row = row == k
        at_lane = inner == k
        pivot_row = jnp.sum(jnp.where(at_row, work, 0.0), axis=0, keepdims=True)
        picked = jnp.where(at_lane, work, 0.0)
        col_out = jnp.sum(jnp.where(left, picked, 0.0), axis=1, keepdims=True)
        col_in = jnp.sum(jnp.where(left, 0.0, picked), axis=1, keepdims=True)
        column = jnp.where(left, col_out, col_in)
        pivot = jnp.sum(jnp.where(at_row, column, 0.0), axis=0, keepdims=True)
        inv = 1.0 / pivot
        scaled = pivot_row * inv
        body = jnp.where(at_lane, 0.0, work) - column * jnp.where(at_lane, inv, scaled)
        top = jnp.where(at_lane, inv, scaled)
        return jnp.where(at_row, top, body)

    out[...] = lax.fori_loop(0, 64, step, work)


def full(shape, dtype=F32):
    return jax.ShapeDtypeStruct(shape, dtype)


VMEM = pl.BlockSpec(memory_space=pltpu.VMEM)
SMEM = pl.BlockSpec(memory_space=pltpu.SMEM)
ANY = pl.BlockSpec(memory_space=pl.ANY)


def per_device(hidden, head_weight, in_proj, out_proj, targets, lengths, grad_store):
    token_count, width = hidden.shape
    x, z = lax.axis_index("x"), lax.axis_index("z")
    rows = lax.axis_index("y") * NC + lax.axis_index("c")
    place = jnp.stack([x, z, rows * NX + x]).astype(jnp.int32)
    head = lax.all_gather(head_weight, ("y", "c"), axis=0, tiled=True)
    mine = spread(hidden.T, "x", NX).reshape(NX * width, token_count).T
    chunks, offsets = [mine], [0]
    up = down = mine
    for k in range(1, NZ // 2):
        up, down = shift(up, "z", 1, NZ), shift(down, "z", -1, NZ)
        chunks += [up, down]
        offsets += [-k, k]
    chunks.append(shift(up, "z", 1, NZ))
    offsets.append(-(NZ // 2))
    count = len(chunks)
    features = head.shape[0]
    packed, proj = pl.pallas_call(
        functools.partial(logits_kernel, offsets),
        out_shape=(full((NX, 2 * TILE, TILE)), full((TILE, 64))),
        in_specs=[SMEM] + [ANY] * count + [ANY, VMEM, VMEM, VMEM],
        out_specs=(VMEM, VMEM),
        scratch_shapes=[
            pltpu.VMEM((token_count, features), BF16),
            pltpu.VMEM((features, head.shape[1]), BF16),
            pltpu.VMEM((features, 64), BF16),
            pltpu.VMEM((token_count, head.shape[1]), F32),
            pltpu.SemaphoreType.DMA((count * (NX + 1),)),
        ],
        name="logits",
    )(place, *chunks, head, in_proj, out_proj, targets[:, None])
    merged = pl.pallas_call(
        merge_x_kernel,
        out_shape=full((NZ, 2 * TILE // NZ, TILE)),
        in_specs=[VMEM],
        out_specs=VMEM,
        name="merge_x",
    )(exchange(packed, "x"))
    grad = pl.pallas_call(
        merge_z_kernel,
        out_shape=full((TILE // NZ, TILE)),
        in_specs=[VMEM],
        out_specs=VMEM,
        name="merge_z",
    )(exchange(merged, "z"))
    gram = pl.pallas_call(
        gram_kernel,
        out_shape=full((96, TILE)),
        in_specs=[SMEM, SMEM, VMEM, VMEM],
        out_specs=VMEM,
        name="gram",
    )(place, lengths, spread(grad, "z", NZ), proj)
    grams = spread(gram, ("x", "y", "c"), NX * NY * NC)
    inverses = pl.pallas_call(
        inverse_kernel,
        out_shape=full((64, TILE)),
        in_specs=[SMEM, VMEM],
        out_specs=VMEM,
        name="inverse",
    )(lengths, grams)
    seq_grads = grams.reshape(NX, NY * NC, 96, TILE)[:, :, :64, 64:]
    seq_grads = jnp.transpose(seq_grads, (1, 0, 2, 3)).reshape(NX * NY * NC, 64, 64)
    half = jnp.einsum("skj,jl->skl", seq_grads, inverses[:, 64:], precision=HI)
    whitened = jnp.einsum("ik,skl->sil", inverses[:, :64], half, precision=HI)
    whitened = whitened.reshape(NX * NY * NC, 64 * 64).astype(BF16)
    return jnp.dot(whitened, grad_store.T, preferred_element_type=F32)


def solution(mesh):
    grid = Mesh(mesh.devices.reshape(NX, NZ, NY, NC), ("x", "z", "y", "c"))
    return jax.shard_map(
        per_device,
        mesh=grid,
        in_specs=(
            P(("y", "c"), ("x", "z")),
            P(("y", "c"), ("x", "z")),
            P(),
            P(("x", "z"), None),
            P(("y", "c")),
            P(),
            P(("x", "z", "y", "c"), None),
        ),
        out_specs=P(None, ("x", "z", "y", "c")),
        check_vma=False,
    )
```

```python
import functools
import jax
import jax.numpy as jnp
from jax import lax
from jax.experimental import pallas as pl
from jax.experimental.pallas import tpu as pltpu
from jax.sharding import Mesh, PartitionSpec as P

TILE = 128
NX, NZ, NY, NC = 4, 16, 4, 2
ZH, ZL = 4, 4
HALF = 32
ROWS = TILE // ZL
STEPS = (0, -1, 1, -2)
BLOCK = 256

damping_ratio = 0.1
tiny_value = 1e-06
HI = lax.Precision.HIGHEST
F32 = jnp.float32
BF16 = jnp.bfloat16


def shift(value, axis, step, size):
    return lax.ppermute(value, axis, [(i, (i + step) % size) for i in range(size)])


def spread(value, axis, size):
    copies = jnp.broadcast_to(value[None], (size,) + value.shape)
    return lax.all_to_all(copies, axis, 0, 0, tiled=True)


def fetch(kinds, chunks, head, in_proj, x, z, feat_buf, head_buf, proj_buf, sems):
    copies = []
    for j, (kind, step) in enumerate(kinds):
        width = chunks[j].shape[1]
        copy = pltpu.make_async_copy(chunks[j], feat_buf.at[:, pl.ds(j * width, width)], sems.at[j, 0])
        copy.start()
        copies.append(copy)
        for a in range(4):
            for i in range(ZH):
                if kind == "x":
                    xs, zs, low = (x + step + NX) % NX, (z + STEPS[a] + NZ) % ZL, 0
                else:
                    xs, zs, low = a, (z + step + NZ) % ZL, HALF
                first = pl.multiple_of(xs * (NZ * 2 * HALF) + (i * ZL + zs) * (2 * HALF) + low, HALF)
                place = j * width + (a * ZH + i) * HALF
                copy = pltpu.make_async_copy(
                    head.at[pl.ds(first, HALF), :], head_buf.at[pl.ds(place, HALF), :], sems.at[j, 1 + a * ZH + i]
                )
                copy.start()
                copies.append(copy)
                proj_buf[pl.ds(place, HALF), :] = in_proj[pl.ds(first, HALF), :]
    for copy in copies:
        copy.wait()


def first_kernel(kinds, place_ref, *refs):
    count = len(kinds)
    chunks = refs[:count]
    head, in_proj, acc, proj = refs[count : count + 4]
    feat_buf, head_buf, proj_buf, sems = refs[count + 4 :]
    x, z = place_ref[0], place_ref[1]
    fetch(kinds, chunks, head, in_proj, x, z, feat_buf, head_buf, proj_buf, sems)

    def column_block(n, carry):
        cols = pl.ds(pl.multiple_of(n * BLOCK, BLOCK), BLOCK)
        acc[:, cols] = jnp.dot(feat_buf[...], head_buf[:, cols], preferred_element_type=F32)
        return carry

    lax.fori_loop(0, acc.shape[1] // BLOCK, column_block, 0)
    own = pl.ds(pl.multiple_of(x * TILE, TILE), TILE)
    proj[...] = jnp.dot(feat_buf[own, :], proj_buf[...], preferred_element_type=F32)


def stat_tile(peak, total, rows):
    lane = lax.broadcasted_iota(jnp.int32, (rows, TILE), 1)
    stat = jnp.where(lane == 0, peak, jnp.where(lane == 1, total, 0.0))
    if rows < TILE:
        stat = jnp.concatenate([stat, jnp.zeros((TILE - rows, TILE), F32)], axis=0)
    return stat.T[0:8, :]


def logits_kernel(kinds, place_ref, *refs):
    count = len(kinds)
    chunks = refs[:count]
    head, in_proj, acc, proj_in, out_proj, targets, packed, proj = refs[count : count + 8]
    feat_buf, head_buf, proj_buf, logit_buf, sems = refs[count + 8 :]
    x, z = place_ref[0], place_ref[1]
    fetch(kinds, chunks, head, in_proj, x, z, feat_buf, head_buf, proj_buf, sems)
    total_cols = head.shape[1]

    def column_block(n, carry):
        cols = pl.ds(pl.multiple_of(n * BLOCK, BLOCK), BLOCK)
        logit_buf[:, cols] = acc[:, cols] + jnp.dot(feat_buf[...], head_buf[:, cols], preferred_element_type=F32)
        return carry

    lax.fori_loop(0, total_cols // BLOCK, column_block, 0)
    own = pl.ds(pl.multiple_of(x * TILE, TILE), TILE)
    proj[...] = proj_in[...] + jnp.dot(feat_buf[own, :], proj_buf[...], preferred_element_type=F32)
    table = out_proj[...]
    vocab_first = (x * NZ + z) * total_cols

    def row_block(i, carry):
        rows = pl.ds(pl.multiple_of(i * TILE, TILE), TILE)
        logits = logit_buf[rows, :]
        peak = jnp.max(logits, axis=1, keepdims=True)
        weight = jnp.exp(logits - peak)
        total = jnp.sum(weight, axis=1, keepdims=True)
        part1 = weight.astype(BF16)
        rest = weight - part1.astype(F32)
        part2 = rest.astype(BF16)
        part3 = (rest - part2.astype(F32)).astype(BF16)
        mixed = jnp.dot(part1, table, preferred_element_type=F32)
        mixed += jnp.dot(part2, table, preferred_element_type=F32)
        mixed += jnp.dot(part3, table, preferred_element_type=F32)
        column = lax.broadcasted_iota(jnp.int32, logits.shape, 1) + vocab_first
        hit = jnp.where(column == targets[rows, :], 1.0, 0.0).astype(BF16)
        picked = jnp.dot(hit, table, preferred_element_type=F32)
        data = jnp.concatenate([mixed, picked], axis=1)
        stat = stat_tile(peak, total, TILE)
        for b in range(ZL):
            packed[i * ZL + b, 0:ROWS, :] = data[b * ROWS : (b + 1) * ROWS, :]
            packed[i * ZL + b, ROWS : ROWS + 8, :] = stat
        return carry

    lax.fori_loop(0, NX, row_block, 0)


def merge(parts):
    peak = functools.reduce(jnp.maximum, [p for _, p, _ in parts])
    scales = [jnp.exp(p - peak) for _, p, _ in parts]
    total = sum(s * t for s, (_, _, t) in zip(scales, parts))
    mixed = sum(s * data[:, :64] for s, (data, _, _) in zip(scales, parts))
    picked = sum(data[:, 64:] for data, _, _ in parts)
    return mixed, picked, peak, total


def merge_kernel(place_ref, packed, out, turned):
    low = place_ref[1] % ZL
    count = packed.shape[0]
    turned[...] = packed[:, ROWS : ROWS + 8, :].reshape(count * 8, TILE).T
    stat = turned[pl.ds(pl.multiple_of(low * ROWS, ROWS), ROWS), :]
    parts = [(packed[i, 0:ROWS, :], stat[:, 8 * i : 8 * i + 1], stat[:, 8 * i + 1 : 8 * i + 2]) for i in range(count)]
    mixed, picked, peak, total = merge(parts)
    out[0:ROWS, :] = jnp.concatenate([mixed, picked], axis=1)
    out[ROWS : ROWS + 8, :] = stat_tile(peak, total, ROWS)


def gram_kernel(place_ref, lengths, packed, proj, out):
    stat = packed[:, ROWS : ROWS + 8, :].reshape(NZ * 8, TILE).T[0:ROWS, :]
    blocks = []
    for b in range(ZL):
        parts = []
        for i in range(ZH):
            at = i * ZL + b
            parts.append((packed[at, 0:ROWS, :], stat[:, 8 * at : 8 * at + 1], stat[:, 8 * at + 1 : 8 * at + 2]))
        mixed, picked, _, total = merge(parts)
        blocks.append(mixed / total - picked)
    length = lengths[place_ref[2]]
    both = jnp.concatenate([jnp.concatenate(blocks, axis=0), proj[...]], axis=1)
    row = lax.broadcasted_iota(jnp.int32, both.shape, 0)
    both = jnp.where(row < length, both, 0.0)
    gram = lax.dot_general(both, both, (((0,), (0,)), ((), ())), precision=HI, preferred_element_type=F32)
    row = lax.broadcasted_iota(jnp.int32, (64, 64), 0)
    col = lax.broadcasted_iota(jnp.int32, (64, 64), 1)
    cov_in = gram[64:128, 64:128]
    root = jnp.sqrt(jnp.full((64, 64), length.astype(F32)))
    out[0:64, :] = jnp.concatenate(
        [jnp.where(row <= col, gram[0:64, 0:64], cov_in), gram[0:64, 64:128] / root], axis=1
    )
    diag = jnp.sum(jnp.where(row == col, cov_in, 0.0), axis=0, keepdims=True)
    out[64:72, :] = jnp.broadcast_to(jnp.concatenate([diag, diag], axis=1), (8, TILE))


def whiten_kernel(lengths, grams, out):
    total = functools.reduce(jnp.add, [lengths[s] for s in range(lengths.shape[0])]).astype(F32)
    summed = functools.reduce(jnp.add, [grams[d] for d in range(grams.shape[0])]) / total
    row = lax.broadcasted_iota(jnp.int32, (64, TILE), 0)
    lane = lax.broadcasted_iota(jnp.int32, (64, TILE), 1)
    left = lane < 64
    inner = jnp.where(left, lane, lane - 64)
    block = jnp.where(left, summed[0:64, :], 0.0)
    turned = jnp.concatenate([block, jnp.zeros_like(block)], axis=0).T[0:64, :]
    upper, lower = row < inner, row > inner
    cov_out = jnp.where(lower, turned, block)[:, 0:64]
    cov_in = jnp.where(upper, turned, block)[:, 0:64]
    work = jnp.concatenate([cov_out, cov_in], axis=1)
    on_diag = row == inner
    work = jnp.where(on_diag & (lane >= 64), summed[64:65, :], work)
    diag = jnp.where(on_diag, work, 0.0)
    trace_out = jnp.sum(jnp.where(left, diag, 0.0))
    trace_in = jnp.sum(jnp.where(left, 0.0, diag))
    damp = jnp.where(left, damping_ratio * trace_out / 64 + tiny_value, damping_ratio * trace_in / 64 + tiny_value)
    work = work + jnp.where(on_diag, damp, 0.0)
    for k in range(64):
        at_lane = inner == k
        pivot_row = work[k : k + 1, :]
        column = jnp.where(left, work[:, k : k + 1], work[:, 64 + k : 65 + k])
        inv = 1.0 / column[k : k + 1, :]
        scaled = jnp.where(at_lane[0:1, :], inv, pivot_row * inv)
        body = jnp.where(at_lane, 0.0, work) - column * scaled
        work = jnp.where(row == k, scaled, body)
    inv_out, inv_in = work[:, 0:64], work[:, 64:128]
    zero = jnp.zeros((64, 64), F32)
    twice = jnp.concatenate(
        [jnp.concatenate([inv_in, zero], axis=1), jnp.concatenate([zero, inv_in], axis=1)], axis=0
    )
    pairs = []
    for s in range(0, grams.shape[0], 2):
        at = [(q % NX) * (NY * NC) + q // NX for q in (s, s + 1)]
        pairs.append(jnp.concatenate([grams[at[0], 0:64, 64:128], grams[at[1], 0:64, 64:128]], axis=1))
    half = jnp.dot(jnp.concatenate(pairs, axis=0), twice, precision=HI, preferred_element_type=F32)
    half = jnp.concatenate([half[64 * p : 64 * p + 64, :] for p in range(len(pairs))], axis=1)
    out[...] = jnp.dot(inv_out, half, precision=HI, preferred_element_type=F32).astype(BF16)


def full(shape, dtype=F32):
    return jax.ShapeDtypeStruct(shape, dtype)


VMEM = pl.BlockSpec(memory_space=pltpu.VMEM)
SMEM = pl.BlockSpec(memory_space=pltpu.SMEM)
ANY = pl.BlockSpec(memory_space=pl.ANY)
ZAXIS = ("zh", "zl")


def per_device(hidden, head_weight, in_proj, out_proj, targets, lengths, grad_store):
    token_count, width = hidden.shape
    x = lax.axis_index("x")
    z = lax.axis_index("zh") * ZL + lax.axis_index("zl")
    rows = lax.axis_index("y") * NC + lax.axis_index("c")
    place = jnp.stack([x, z, rows * NX + x]).astype(jnp.int32)
    head = lax.all_gather(head_weight, ("y", "c"), axis=0, tiled=True)
    strided = spread(hidden.T, "zh", ZH)
    a_own = strided[:, :HALF, :].reshape(ZH * HALF, token_count).T
    a_parts = [a_own] + [shift(a_own, ZAXIS, -s, NZ) for s in STEPS[1:]]
    b_own = spread(strided[:, HALF:, :].reshape(ZH * HALF, token_count), "x", NX)
    b_own = b_own.reshape(NX * ZH * HALF, token_count).T
    a_own = jnp.concatenate(a_parts, axis=1)
    b_back, b_next = shift(b_own, ZAXIS, 1, NZ), shift(b_own, ZAXIS, -1, NZ)
    a_back, a_next = shift(a_own, "x", 1, NX), shift(a_own, "x", -1, NX)
    b_far, a_far = shift(b_back, ZAXIS, 1, NZ), shift(a_back, "x", 1, NX)
    cols = head.shape[1]
    size = a_own.shape[1]

    def buffers(count):
        return [
            pltpu.VMEM((token_count, count * size), BF16),
            pltpu.VMEM((count * size, cols), BF16),
            pltpu.VMEM((count * size, 64), BF16),
        ]

    early = (("x", 0), ("z", 0), ("x", -1), ("x", 1), ("z", -1), ("z", 1))
    acc, proj = pl.pallas_call(
        functools.partial(first_kernel, early),
        out_shape=(full((token_count, cols)), full((TILE, 64))),
        in_specs=[SMEM] + [ANY] * len(early) + [ANY, VMEM],
        out_specs=(VMEM, VMEM),
        scratch_shapes=buffers(len(early)) + [pltpu.SemaphoreType.DMA((len(early), 17))],
        name="logits_first",
    )(place, a_own, b_own, a_back, a_next, b_back, b_next, head, in_proj)
    late = (("x", -2), ("z", -2))
    packed, proj = pl.pallas_call(
        functools.partial(logits_kernel, late),
        out_shape=(full((NX * ZL, ROWS + 8, TILE)), full((TILE, 64))),
        in_specs=[SMEM] + [ANY] * len(late) + [ANY] + [VMEM] * 5,
        out_specs=(VMEM, VMEM),
        scratch_shapes=buffers(len(late))
        + [pltpu.VMEM((token_count, cols), F32), pltpu.SemaphoreType.DMA((len(late), 17))],
        name="logits_last",
    )(place, a_far, b_far, head, in_proj, acc, proj, out_proj, targets[:, None])
    merged = pl.pallas_call(
        merge_kernel,
        out_shape=full((ROWS + 8, TILE)),
        in_specs=[SMEM, VMEM],
        out_specs=VMEM,
        scratch_shapes=[pltpu.VMEM((TILE, TILE), F32)],
        name="merge",
    )(place, lax.all_to_all(packed, ("x", "zl"), 0, 0, tiled=True))
    gram = pl.pallas_call(
        gram_kernel,
        out_shape=full((72, TILE)),
        in_specs=[SMEM, SMEM, VMEM, VMEM],
        out_specs=VMEM,
        name="gram",
    )(place, lengths, spread(merged, ZAXIS, NZ), proj)
    seqs = NX * NY * NC
    grams = spread(gram, ("x", "y", "c"), seqs)
    whitened = pl.pallas_call(
        whiten_kernel,
        out_shape=full((64, seqs * 64), BF16),
        in_specs=[SMEM, VMEM],
        out_specs=VMEM,
        name="whiten",
    )(lengths, grams)
    whitened = jnp.transpose(whitened.reshape(64, seqs, 64), (1, 0, 2)).reshape(seqs, 64 * 64)
    return jnp.dot(whitened, grad_store.T, preferred_element_type=F32)


def solution(mesh):
    grid = Mesh(mesh.devices.reshape(NX, ZH, ZL, NY, NC), ("x", "zh", "zl", "y", "c"))
    return jax.shard_map(
        per_device,
        mesh=grid,
        in_specs=(
            P(("y", "c"), ("x", "zh", "zl")),
            P(("y", "c"), ("x", "zh", "zl")),
            P(),
            P(("x", "zh", "zl"), None),
            P(("y", "c")),
            P(),
            P(("x", "zh", "zl", "y", "c"), None),
        ),
        out_specs=P(None, ("x", "zh", "zl", "y", "c")),
        check_vma=False,
    )
```

```python
import functools
import jax
import jax.numpy as jnp
from jax import lax
from jax.experimental import pallas as pl
from jax.experimental.pallas import tpu as pltpu
from jax.sharding import Mesh, PartitionSpec as P

TILE = 128
NX, NZ, NY, NC = 4, 16, 4, 2
ZH, ZL = 4, 4
HALF = 32
ROWS = TILE // ZL
STEPS = (0, -1, 1, -2)
BLOCK = 1024
UNROLL = 4
EARLY, LATE = (0, 4, 1, 2, 5, 6), (3, 7)

damping_ratio = 0.1
tiny_value = 1e-06
HI = lax.Precision.HIGHEST
F32 = jnp.float32
BF16 = jnp.bfloat16


def shift(value, axis, step, size):
    return lax.ppermute(value, axis, [(i, (i + step) % size) for i in range(size)])


def spread(value, axis, size):
    copies = jnp.broadcast_to(value[None], (size,) + value.shape)
    return lax.all_to_all(copies, axis, 0, 0, tiled=True)


def exchange(value, axis):
    return lax.all_to_all(value, axis, 0, 0, tiled=True)


def prepare_kernel(place_ref, in_proj, out_proj, targets, picked, in_copy, out_copy):
    x, z = place_ref[0], place_ref[1]
    table = out_proj[...]
    cols = table.shape[0]
    column = lax.broadcasted_iota(jnp.int32, (targets.shape[0], cols), 1) + (x * NZ + z) * cols
    hit = jnp.where(column == targets[...], 1.0, 0.0).astype(BF16)
    picked[...] = jnp.dot(hit, table, preferred_element_type=F32)
    in_copy[...] = in_proj[...]
    out_copy[...] = table


def stat_tile(peak, total, rows):
    lane = lax.broadcasted_iota(jnp.int32, (rows, TILE), 1)
    stat = jnp.where(lane == 0, peak, jnp.where(lane == 1, total, 0.0))
    if rows < TILE:
        stat = jnp.concatenate([stat, jnp.zeros((TILE - rows, TILE), F32)], axis=0)
    return stat.T[0:8, :]


def fetch(js, chunks, head, in_proj, x, z, feat_buf, head_buf, proj_buf, sems):
    waits, late_waits = [], []
    for at, j in enumerate(js):
        step = STEPS[j % len(STEPS)]
        copies = [pltpu.make_async_copy(chunks[at], feat_buf.at[at], sems.at[at, 0])]
        others = []
        if j < len(STEPS):
            xs = (x + step + NX) % NX
            for a in range(ZL):
                zs = (z + STEPS[a] + NZ) % ZL
                copies.append(pltpu.make_async_copy(head.at[xs, :, zs, 0], head_buf.at[at, a], sems.at[at, 1 + a]))
                others.append(pltpu.make_async_copy(in_proj.at[xs, :, zs, 0], proj_buf.at[at, a], sems.at[at, 5 + a]))
        else:
            zs = (z + step + NZ) % ZL
            copies.append(pltpu.make_async_copy(head.at[:, :, zs, 1], head_buf.at[at], sems.at[at, 1]))
            others.append(pltpu.make_async_copy(in_proj.at[:, :, zs, 1], proj_buf.at[at], sems.at[at, 5]))
        for copy in copies:
            copy.start()
        waits.append(copies)
        late_waits += others
    for copy in late_waits:
        copy.start()
    return waits, late_waits


def add_products(waits, feat_buf, head_buf, out, ready=None, then=None):
    count, width = feat_buf.shape[0], feat_buf.shape[2]
    for g in range(0, count, 2):
        for copy in waits[g] + waits[g + 1]:
            copy.wait()
        if g == 0 and ready is not None:
            ready.wait()

        def column_block(n, carry, g=g):
            at = pl.ds(pl.multiple_of(n * BLOCK, BLOCK), BLOCK)
            part = None if g == 0 and ready is None else out[:, at]
            for j in (g, g + 1):
                more = jnp.dot(feat_buf[j], head_buf[j, :, :, :, at].reshape(width, BLOCK), preferred_element_type=F32)
                part = more if part is None else part + more
            out[:, at] = part
            if then is not None and g + 2 == count:
                then(n, at).start()
            return carry

        lax.fori_loop(0, out.shape[1] // BLOCK, column_block, 0)


def project(feat_buf, proj_buf, x, waits):
    own = pl.ds(pl.multiple_of(x * TILE, TILE), TILE)
    for copy in waits:
        copy.wait()
    return sum(
        jnp.dot(feat_buf[j, own, :], proj_buf[j].reshape(feat_buf.shape[2], 64), preferred_element_type=F32)
        for j in range(feat_buf.shape[0])
    )


def first_kernel(place_ref, *refs):
    chunks = refs[: len(EARLY)]
    head, in_proj, acc, proj, feat_buf, head_buf, proj_buf, sems, acc_buf, out_sems = refs[len(EARLY) :]
    x, z = place_ref[0], place_ref[1]
    waits, others = fetch(EARLY, chunks, head, in_proj, x, z, feat_buf, head_buf, proj_buf, sems)

    def store(n, at):
        return pltpu.make_async_copy(acc_buf.at[:, at], acc.at[:, at], out_sems.at[n])

    add_products(waits, feat_buf, head_buf, acc_buf, then=store)
    proj[...] = project(feat_buf, proj_buf, x, others)
    for n in range(acc_buf.shape[1] // BLOCK):
        store(n, pl.ds(n * BLOCK, BLOCK)).wait()


def logits_kernel(place_ref, *refs):
    chunks = refs[: len(LATE)]
    head, in_proj, acc, proj_in, out_proj, picked, packed, proj = refs[len(LATE) : len(LATE) + 8]
    feat_buf, head_buf, proj_buf, sems, logit_buf, in_sem = refs[len(LATE) + 8 :]
    x, z = place_ref[0], place_ref[1]
    waits, others = fetch(LATE, chunks, head, in_proj, x, z, feat_buf, head_buf, proj_buf, sems)
    ready = pltpu.make_async_copy(acc, logit_buf, in_sem)
    ready.start()
    add_products(waits, feat_buf, head_buf, logit_buf, ready=ready)
    proj[...] = proj_in[...] + project(feat_buf, proj_buf, x, others)
    table = out_proj[...]

    def row_block(i, carry):
        rows = pl.ds(pl.multiple_of(i * TILE, TILE), TILE)
        logits = logit_buf[rows, :]
        peak = jnp.max(logits, axis=1, keepdims=True)
        weight = jnp.exp(logits - peak)
        total = jnp.sum(weight, axis=1, keepdims=True)
        part1 = weight.astype(BF16)
        rest = weight - part1.astype(F32)
        part2 = rest.astype(BF16)
        part3 = (rest - part2.astype(F32)).astype(BF16)
        mixed = jnp.dot(part1, table, preferred_element_type=F32)
        mixed += jnp.dot(part2, table, preferred_element_type=F32)
        mixed += jnp.dot(part3, table, preferred_element_type=F32)
        data = jnp.concatenate([mixed, picked[rows, :]], axis=1)
        stat = stat_tile(peak, total, TILE)
        for b in range(ZL):
            packed[i * ZL + b, 0:ROWS, :] = data[b * ROWS : (b + 1) * ROWS, :]
            packed[i * ZL + b, ROWS : ROWS + 8, :] = stat
        return carry

    lax.fori_loop(0, NX, row_block, 0, unroll=UNROLL)


def merge(parts):
    peak = functools.reduce(jnp.maximum, [p for _, p, _ in parts])
    scales = [jnp.exp(p - peak) for _, p, _ in parts]
    total = sum(s * t for s, (_, _, t) in zip(scales, parts))
    mixed = sum(s * data[:, :64] for s, (data, _, _) in zip(scales, parts))
    picked = sum(data[:, 64:] for data, _, _ in parts)
    return mixed, picked, peak, total


def merge_kernel(place_ref, packed, out, turned):
    low = place_ref[1] % ZL
    count = packed.shape[0]
    turned[...] = packed[:, ROWS : ROWS + 8, :].reshape(count * 8, TILE).T
    stat = turned[pl.ds(pl.multiple_of(low * ROWS, ROWS), ROWS), :]
    parts = [(packed[i, 0:ROWS, :], stat[:, 8 * i : 8 * i + 1], stat[:, 8 * i + 1 : 8 * i + 2]) for i in range(count)]
    mixed, picked, peak, total = merge(parts)
    data, stat = jnp.concatenate([mixed, picked], axis=1), stat_tile(peak, total, ROWS)
    for i in range(NZ):
        out[i, 0:ROWS, :] = data
        out[i, ROWS : ROWS + 8, :] = stat


def gram_kernel(place_ref, lengths, packed, proj, out):
    stat = packed[:, ROWS : ROWS + 8, :].reshape(NZ * 8, TILE).T[0:ROWS, :]
    blocks = []
    for b in range(ZL):
        parts = []
        for i in range(ZH):
            at = i * ZL + b
            parts.append((packed[at, 0:ROWS, :], stat[:, 8 * at : 8 * at + 1], stat[:, 8 * at + 1 : 8 * at + 2]))
        mixed, picked, _, total = merge(parts)
        blocks.append(mixed / total - picked)
    length = lengths[place_ref[2]]
    both = jnp.concatenate([jnp.concatenate(blocks, axis=0), proj[...]], axis=1)
    row = lax.broadcasted_iota(jnp.int32, both.shape, 0)
    both = jnp.where(row < length, both, 0.0)
    gram = lax.dot_general(both, both, (((0,), (0,)), ((), ())), precision=HI, preferred_element_type=F32)
    row = lax.broadcasted_iota(jnp.int32, (64, 64), 0)
    col = lax.broadcasted_iota(jnp.int32, (64, 64), 1)
    cov_in = gram[64:128, 64:128]
    root = jnp.sqrt(jnp.full((64, 64), length.astype(F32)))
    data = jnp.concatenate([jnp.where(row <= col, gram[0:64, 0:64], cov_in), gram[0:64, 64:128] / root], axis=1)
    diag = jnp.sum(jnp.where(row == col, cov_in, 0.0), axis=0, keepdims=True)
    diag = jnp.broadcast_to(jnp.concatenate([diag, diag], axis=1), (8, TILE))
    for i in range(out.shape[0]):
        out[i, 0:64, :] = data
        out[i, 64:72, :] = diag


def whiten_kernel(lengths, grams, out):
    total = functools.reduce(jnp.add, [lengths[s] for s in range(lengths.shape[0])]).astype(F32)
    summed = functools.reduce(jnp.add, [grams[d] for d in range(grams.shape[0])]) / total
    row = lax.broadcasted_iota(jnp.int32, (64, TILE), 0)
    lane = lax.broadcasted_iota(jnp.int32, (64, TILE), 1)
    left = lane < 64
    inner = jnp.where(left, lane, lane - 64)
    block = jnp.where(left, summed[0:64, :], 0.0)
    turned = jnp.concatenate([block, jnp.zeros_like(block)], axis=0).T[0:64, :]
    upper, lower = row < inner, row > inner
    cov_out = jnp.where(lower, turned, block)[:, 0:64]
    cov_in = jnp.where(upper, turned, block)[:, 0:64]
    work = jnp.concatenate([cov_out, cov_in], axis=1)
    on_diag = row == inner
    work = jnp.where(on_diag & (lane >= 64), summed[64:65, :], work)
    diag = jnp.where(on_diag, work, 0.0)
    trace_out = jnp.sum(jnp.where(left, diag, 0.0))
    trace_in = jnp.sum(jnp.where(left, 0.0, diag))
    damp = jnp.where(left, damping_ratio * trace_out / 64 + tiny_value, damping_ratio * trace_in / 64 + tiny_value)
    work = work + jnp.where(on_diag, damp, 0.0)
    def column(work, k):
        return jnp.where(left, work[:, k : k + 1], work[:, 64 + k : 65 + k])

    for k in range(0, 64, 2):
        at0, at1 = inner == k, inner == k + 1
        row0, row1 = work[k : k + 1, :], work[k + 1 : k + 2, :]
        col0, col1 = column(work, k), column(work, k + 1)
        p00, p01 = col0[k : k + 1, :], col1[k : k + 1, :]
        p10, p11 = col0[k + 1 : k + 2, :], col1[k + 1 : k + 2, :]
        inv = 1.0 / (p00 * p11 - p01 * p10)
        q00, q01, q10, q11 = p11 * inv, -p01 * inv, -p10 * inv, p00 * inv
        new0, new1 = q00 * row0 + q01 * row1, q10 * row0 + q11 * row1
        new0 = jnp.where(at0[0:1, :], q00, jnp.where(at1[0:1, :], q01, new0))
        new1 = jnp.where(at0[0:1, :], q10, jnp.where(at1[0:1, :], q11, new1))
        body = jnp.where(at0 | at1, 0.0, work) - col0 * new0 - col1 * new1
        work = jnp.where(row == k, new0, jnp.where(row == k + 1, new1, body))
    inv_out, inv_in = work[:, 0:64], work[:, 64:128]
    zero = jnp.zeros((64, 64), F32)
    twice = jnp.concatenate(
        [jnp.concatenate([inv_in, zero], axis=1), jnp.concatenate([zero, inv_in], axis=1)], axis=0
    )
    pairs = []
    for s in range(0, grams.shape[0], 2):
        at = [(q % NX) * (NY * NC) + q // NX for q in (s, s + 1)]
        pairs.append(jnp.concatenate([grams[at[0], 0:64, 64:128], grams[at[1], 0:64, 64:128]], axis=1))
    half = jnp.dot(jnp.concatenate(pairs, axis=0), twice, precision=HI, preferred_element_type=F32)
    half = jnp.concatenate([half[64 * p : 64 * p + 64, :] for p in range(len(pairs))], axis=1)
    full_white = jnp.dot(inv_out, half, precision=HI, preferred_element_type=F32)
    for s in range(grams.shape[0]):
        out[s] = full_white[:, 64 * s : 64 * s + 64].astype(BF16)


def full(shape, dtype=F32):
    return jax.ShapeDtypeStruct(shape, dtype)


VMEM = pl.BlockSpec(memory_space=pltpu.VMEM)
SMEM = pl.BlockSpec(memory_space=pltpu.SMEM)
ANY = pl.BlockSpec(memory_space=pl.ANY)
ZAXIS = ("zh", "zl")


def per_device(hidden, head_weight, in_proj, out_proj, targets, lengths, grad_store):
    token_count, width = hidden.shape
    x = lax.axis_index("x")
    z = lax.axis_index("zh") * ZL + lax.axis_index("zl")
    rows = lax.axis_index("y") * NC + lax.axis_index("c")
    place = jnp.stack([x, z, rows * NX + x]).astype(jnp.int32)
    cols = head_weight.shape[1]
    head = lax.all_gather(head_weight, ("y", "c"), axis=0, tiled=True)
    picked, in_rows, out_rows = pl.pallas_call(
        prepare_kernel,
        out_shape=(full((token_count, 64)), full(in_proj.shape, BF16), full(out_proj.shape, BF16)),
        in_specs=[SMEM, VMEM, VMEM, VMEM],
        out_specs=(VMEM, VMEM, VMEM),
        name="prepare",
    )(place, in_proj, out_proj, targets[:, None])
    strided = spread(hidden.T, "zh", ZH)
    strided, picked, in_rows, out_rows = lax.optimization_barrier((strided, picked, in_rows, out_rows))
    size = NX * ZH * HALF
    a_own = strided[:, :HALF, :].reshape(ZH * HALF, token_count).T
    a_parts = [a_own] + [shift(a_own, ZAXIS, -s, NZ) for s in STEPS[1:]]
    b_own = spread(strided[:, HALF:, :].reshape(ZH * HALF, token_count), "x", NX)
    b_own = b_own.reshape(size, token_count).T
    a_own = jnp.concatenate(a_parts, axis=1)
    b_back, b_next = shift(b_own, ZAXIS, 1, NZ), shift(b_own, ZAXIS, -1, NZ)
    a_back, a_next = shift(a_own, "x", 1, NX), shift(a_own, "x", -1, NX)
    b_far, a_far = shift(b_back, ZAXIS, 1, NZ), shift(a_back, "x", 1, NX)
    chunks = [a_own, a_back, a_next, a_far, b_own, b_back, b_next, b_far]
    head = head.reshape(NX, ZH, ZL, 2, HALF, cols)
    in_rows = in_rows.reshape(NX, ZH, ZL, 2, HALF, 64)

    def buffers(count):
        return [
            pltpu.VMEM((count, token_count, size), BF16),
            pltpu.VMEM((count, NX, ZH, HALF, cols), BF16),
            pltpu.VMEM((count, NX, ZH, HALF, 64), BF16),
            pltpu.SemaphoreType.DMA((count, 1 + 2 * ZL)),
            pltpu.VMEM((token_count, cols), F32),
        ]

    acc, proj = pl.pallas_call(
        first_kernel,
        out_shape=(full((token_count, cols)), full((TILE, 64))),
        in_specs=[SMEM] + [ANY] * (len(EARLY) + 2),
        out_specs=(ANY, VMEM),
        scratch_shapes=buffers(len(EARLY)) + [pltpu.SemaphoreType.DMA((cols // BLOCK,))],
        name="logits_first",
    )(place, *[chunks[j] for j in EARLY], head, in_rows)
    packed, proj = pl.pallas_call(
        logits_kernel,
        out_shape=(full((NX * ZL, ROWS + 8, TILE)), full((TILE, 64))),
        in_specs=[SMEM] + [ANY] * (len(LATE) + 3) + [VMEM] * 3,
        out_specs=(VMEM, VMEM),
        scratch_shapes=buffers(len(LATE)) + [pltpu.SemaphoreType.DMA(())],
        name="logits_last",
    )(place, *[chunks[j] for j in LATE], head, in_rows, acc, proj, out_rows, picked)
    merged = pl.pallas_call(
        merge_kernel,
        out_shape=full((NZ, ROWS + 8, TILE)),
        in_specs=[SMEM, VMEM],
        out_specs=VMEM,
        scratch_shapes=[pltpu.VMEM((TILE, TILE), F32)],
        name="merge",
    )(place, exchange(packed, ("x", "zl")))
    seqs = NX * NY * NC
    gram = pl.pallas_call(
        gram_kernel,
        out_shape=full((seqs, 72, TILE)),
        in_specs=[SMEM, SMEM, VMEM, VMEM],
        out_specs=VMEM,
        name="gram",
    )(place, lengths, exchange(merged, ZAXIS), proj)
    grams = exchange(gram, ("x", "y", "c"))
    whitened = pl.pallas_call(
        whiten_kernel,
        out_shape=full((seqs, 64, 64), BF16),
        in_specs=[SMEM, VMEM],
        out_specs=VMEM,
        name="whiten",
    )(lengths, grams)
    whitened = whitened.reshape(seqs, 64 * 64)
    return jnp.dot(whitened, grad_store.T, preferred_element_type=F32)


def solution(mesh):
    grid = Mesh(mesh.devices.reshape(NX, ZH, ZL, NY, NC), ("x", "zh", "zl", "y", "c"))
    return jax.shard_map(
        per_device,
        mesh=grid,
        in_specs=(
            P(("y", "c"), ("x", "zh", "zl")),
            P(("y", "c"), ("x", "zh", "zl")),
            P(),
            P(("x", "zh", "zl"), None),
            P(("y", "c")),
            P(),
            P(("x", "zh", "zl", "y", "c"), None),
        ),
        out_specs=P(None, ("x", "zh", "zl", "y", "c")),
        check_vma=False,
    )
```

```python
import functools
import jax
import jax.numpy as jnp
from jax import lax
from jax.experimental import pallas as pl
from jax.experimental.pallas import tpu as pltpu
from jax.sharding import Mesh, PartitionSpec as P

TILE = 128
NX, NZ, NY, NC = 4, 16, 4, 2
ZH, ZL = 4, 4
HALF = 32
ROWS = TILE // ZL
STEPS = (0, -1, 1, -2)
BLOCK = 1024
UNROLL = 4
EARLY, LATE = (0, 4, 1, 2, 5, 6), (3, 7)

damping_ratio = 0.1
tiny_value = 1e-06
HI = lax.Precision.HIGHEST
F32 = jnp.float32
BF16 = jnp.bfloat16


def shift(value, axis, step, size):
    return lax.ppermute(value, axis, [(i, (i + step) % size) for i in range(size)])


def spread(value, axis, size):
    copies = jnp.broadcast_to(value[None], (size,) + value.shape)
    return lax.all_to_all(copies, axis, 0, 0, tiled=True)


def exchange(value, axis):
    return lax.all_to_all(value, axis, 0, 0, tiled=True)


def prepare_kernel(place_ref, in_proj, out_proj, targets, picked, in_copy, out_copy):
    x, z = place_ref[0], place_ref[1]
    table = out_proj[...]
    cols = table.shape[0]
    column = lax.broadcasted_iota(jnp.int32, (targets.shape[0], cols), 1) + (x * NZ + z) * cols
    hit = jnp.where(column == targets[...], 1.0, 0.0).astype(BF16)
    picked[...] = jnp.dot(hit, table, preferred_element_type=F32)
    in_copy[...] = in_proj[...]
    out_copy[...] = table


def stat_tile(peak, total, rows):
    lane = lax.broadcasted_iota(jnp.int32, (rows, TILE), 1)
    stat = jnp.where(lane == 0, peak, jnp.where(lane == 1, total, 0.0))
    if rows < TILE:
        stat = jnp.concatenate([stat, jnp.zeros((TILE - rows, TILE), F32)], axis=0)
    return stat.T[0:8, :]


def fetch(js, chunks, head, in_proj, x, z, feat_buf, head_buf, proj_buf, sems):
    waits, late_waits = [], []
    for at, j in enumerate(js):
        step = STEPS[j % len(STEPS)]
        copies = [pltpu.make_async_copy(chunks[at], feat_buf.at[at], sems.at[at, 0])]
        others = []
        if j < len(STEPS):
            xs = (x + step + NX) % NX
            for a in range(ZL):
                zs = (z + STEPS[a] + NZ) % ZL
                copies.append(pltpu.make_async_copy(head.at[xs, :, zs, 0], head_buf.at[at, a], sems.at[at, 1 + a]))
                others.append(pltpu.make_async_copy(in_proj.at[xs, :, zs, 0], proj_buf.at[at, a], sems.at[at, 5 + a]))
        else:
            zs = (z + step + NZ) % ZL
            copies.append(pltpu.make_async_copy(head.at[:, :, zs, 1], head_buf.at[at], sems.at[at, 1]))
            others.append(pltpu.make_async_copy(in_proj.at[:, :, zs, 1], proj_buf.at[at], sems.at[at, 5]))
        for copy in copies:
            copy.start()
        waits.append(copies)
        late_waits += others
    for copy in late_waits:
        copy.start()
    return waits, late_waits


def add_products(waits, feat_buf, head_buf, out, ready=None, then=None):
    count, width = feat_buf.shape[0], feat_buf.shape[2]
    for g in range(0, count, 2):
        for copy in waits[g] + waits[g + 1]:
            copy.wait()
        if g == 0 and ready is not None:
            ready.wait()

        def column_block(n, carry, g=g):
            at = pl.ds(pl.multiple_of(n * BLOCK, BLOCK), BLOCK)
            part = None if g == 0 and ready is None else out[:, at]
            for j in (g, g + 1):
                more = jnp.dot(feat_buf[j], head_buf[j, :, :, :, at].reshape(width, BLOCK), preferred_element_type=F32)
                part = more if part is None else part + more
            out[:, at] = part
            if then is not None and g + 2 == count:
                then(n, at).start()
            return carry

        lax.fori_loop(0, out.shape[1] // BLOCK, column_block, 0)


def project(feat_buf, proj_buf, x, waits):
    own = pl.ds(pl.multiple_of(x * TILE, TILE), TILE)
    for copy in waits:
        copy.wait()
    return sum(
        jnp.dot(feat_buf[j, own, :], proj_buf[j].reshape(feat_buf.shape[2], 64), preferred_element_type=F32)
        for j in range(feat_buf.shape[0])
    )


def first_kernel(place_ref, *refs):
    chunks = refs[: len(EARLY)]
    head, in_proj, acc, proj, feat_buf, head_buf, proj_buf, sems, acc_buf, out_sems = refs[len(EARLY) :]
    x, z = place_ref[0], place_ref[1]
    waits, others = fetch(EARLY, chunks, head, in_proj, x, z, feat_buf, head_buf, proj_buf, sems)

    def store(n, at):
        return pltpu.make_async_copy(acc_buf.at[:, at], acc.at[:, at], out_sems.at[n])

    add_products(waits, feat_buf, head_buf, acc_buf, then=store)
    proj[...] = project(feat_buf, proj_buf, x, others)
    for n in range(acc_buf.shape[1] // BLOCK):
        store(n, pl.ds(n * BLOCK, BLOCK)).wait()


def logits_kernel(place_ref, *refs):
    chunks = refs[: len(LATE)]
    head, in_proj, acc, proj_in, out_proj, picked, packed, proj = refs[len(LATE) : len(LATE) + 8]
    feat_buf, head_buf, proj_buf, sems, logit_buf, in_sem = refs[len(LATE) + 8 :]
    x, z = place_ref[0], place_ref[1]
    waits, others = fetch(LATE, chunks, head, in_proj, x, z, feat_buf, head_buf, proj_buf, sems)
    ready = pltpu.make_async_copy(acc, logit_buf, in_sem)
    ready.start()
    add_products(waits, feat_buf, head_buf, logit_buf, ready=ready)
    proj[...] = proj_in[...] + project(feat_buf, proj_buf, x, others)
    table = out_proj[...]

    def row_block(i, carry):
        rows = pl.ds(pl.multiple_of(i * TILE, TILE), TILE)
        logits = logit_buf[rows, :]
        peak = jnp.max(logits, axis=1, keepdims=True)
        weight = jnp.exp(logits - peak)
        total = jnp.sum(weight, axis=1, keepdims=True)
        part1 = weight.astype(BF16)
        rest = weight - part1.astype(F32)
        part2 = rest.astype(BF16)
        part3 = (rest - part2.astype(F32)).astype(BF16)
        mixed = jnp.dot(part1, table, preferred_element_type=F32)
        mixed += jnp.dot(part2, table, preferred_element_type=F32)
        mixed += jnp.dot(part3, table, preferred_element_type=F32)
        data = jnp.concatenate([mixed, picked[rows, :]], axis=1)
        stat = stat_tile(peak, total, TILE)
        for b in range(ZL):
            packed[i * ZL + b, 0:ROWS, :] = data[b * ROWS : (b + 1) * ROWS, :]
            packed[i * ZL + b, ROWS : ROWS + 8, :] = stat
        return carry

    lax.fori_loop(0, NX, row_block, 0, unroll=UNROLL)


def merge(parts):
    peak = functools.reduce(jnp.maximum, [p for _, p, _ in parts])
    scales = [jnp.exp(p - peak) for _, p, _ in parts]
    total = sum(s * t for s, (_, _, t) in zip(scales, parts))
    mixed = sum(s * data[:, :64] for s, (data, _, _) in zip(scales, parts))
    picked = sum(data[:, 64:] for data, _, _ in parts)
    return mixed, picked, peak, total


def merge_kernel(place_ref, packed, out, turned):
    low = place_ref[1] % ZL
    count = packed.shape[0]
    turned[...] = packed[:, ROWS : ROWS + 8, :].reshape(count * 8, TILE).T
    stat = turned[pl.ds(pl.multiple_of(low * ROWS, ROWS), ROWS), :]
    parts = [(packed[i, 0:ROWS, :], stat[:, 8 * i : 8 * i + 1], stat[:, 8 * i + 1 : 8 * i + 2]) for i in range(count)]
    mixed, picked, peak, total = merge(parts)
    data, stat = jnp.concatenate([mixed, picked], axis=1), stat_tile(peak, total, ROWS)
    for i in range(NZ):
        out[i, 0:ROWS, :] = data
        out[i, ROWS : ROWS + 8, :] = stat


def gram_kernel(place_ref, lengths, packed, proj, out):
    stat = packed[:, ROWS : ROWS + 8, :].reshape(NZ * 8, TILE).T[0:ROWS, :]
    blocks = []
    for b in range(ZL):
        parts = []
        for i in range(ZH):
            at = i * ZL + b
            parts.append((packed[at, 0:ROWS, :], stat[:, 8 * at : 8 * at + 1], stat[:, 8 * at + 1 : 8 * at + 2]))
        mixed, picked, _, total = merge(parts)
        blocks.append(mixed / total - picked)
    length = lengths[place_ref[2]]
    both = jnp.concatenate([jnp.concatenate(blocks, axis=0), proj[...]], axis=1)
    row = lax.broadcasted_iota(jnp.int32, both.shape, 0)
    both = jnp.where(row < length, both, 0.0)
    gram = lax.dot_general(both, both, (((0,), (0,)), ((), ())), precision=HI, preferred_element_type=F32)
    row = lax.broadcasted_iota(jnp.int32, (64, 64), 0)
    col = lax.broadcasted_iota(jnp.int32, (64, 64), 1)
    cov_in = gram[64:128, 64:128]
    root = jnp.sqrt(jnp.full((64, 64), length.astype(F32)))
    data = jnp.concatenate([jnp.where(row <= col, gram[0:64, 0:64], cov_in), gram[0:64, 64:128] / root], axis=1)
    diag = jnp.sum(jnp.where(row == col, cov_in, 0.0), axis=0, keepdims=True)
    diag = jnp.broadcast_to(jnp.concatenate([diag, diag], axis=1), (8, TILE))
    for i in range(out.shape[0]):
        out[i, 0:64, :] = data
        out[i, 64:72, :] = diag


def split_dot(a, b):
    a_top, b_top = a.astype(BF16), b.astype(BF16)
    a_rest, b_rest = (a - a_top.astype(F32)).astype(BF16), (b - b_top.astype(F32)).astype(BF16)
    out = jnp.dot(a_top, b_top, preferred_element_type=F32)
    out += jnp.dot(a_top, b_rest, preferred_element_type=F32)
    return out + jnp.dot(a_rest, b_top, preferred_element_type=F32)


def whiten_kernel(place_ref, lengths, mine, theirs, out):
    total = functools.reduce(jnp.add, [lengths[s] for s in range(lengths.shape[0])]).astype(F32)
    count = mine.shape[0]
    summed = functools.reduce(jnp.add, [mine[d] for d in range(count)])
    summed = (summed + functools.reduce(jnp.add, [theirs[d] for d in range(count)])) / total
    row = lax.broadcasted_iota(jnp.int32, (64, TILE), 0)
    lane = lax.broadcasted_iota(jnp.int32, (64, TILE), 1)
    left = lane < 64
    inner = jnp.where(left, lane, lane - 64)
    block = jnp.where(left, summed[0:64, :], 0.0)
    turned = jnp.concatenate([block, jnp.zeros_like(block)], axis=0).T[0:64, :]
    upper, lower = row < inner, row > inner
    cov_out = jnp.where(lower, turned, block)[:, 0:64]
    cov_in = jnp.where(upper, turned, block)[:, 0:64]
    work = jnp.concatenate([cov_out, cov_in], axis=1)
    on_diag = row == inner
    work = jnp.where(on_diag & (lane >= 64), summed[64:65, :], work)
    diag = jnp.where(on_diag, work, 0.0)
    trace_out = jnp.sum(jnp.where(left, diag, 0.0))
    trace_in = jnp.sum(jnp.where(left, 0.0, diag))
    damp = jnp.where(left, damping_ratio * trace_out / 64 + tiny_value, damping_ratio * trace_in / 64 + tiny_value)
    work = work + jnp.where(on_diag, damp, 0.0)
    def column(work, k):
        return jnp.where(left, work[:, k : k + 1], work[:, 64 + k : 65 + k])

    for k in range(0, 64, 2):
        at0, at1 = inner == k, inner == k + 1
        row0, row1 = work[k : k + 1, :], work[k + 1 : k + 2, :]
        col0, col1 = column(work, k), column(work, k + 1)
        p00, p01 = col0[k : k + 1, :], col1[k : k + 1, :]
        p10, p11 = col0[k + 1 : k + 2, :], col1[k + 1 : k + 2, :]
        inv = 1.0 / (p00 * p11 - p01 * p10)
        q00, q01, q10, q11 = p11 * inv, -p01 * inv, -p10 * inv, p00 * inv
        new0, new1 = q00 * row0 + q01 * row1, q10 * row0 + q11 * row1
        new0 = jnp.where(at0[0:1, :], q00, jnp.where(at1[0:1, :], q01, new0))
        new1 = jnp.where(at0[0:1, :], q10, jnp.where(at1[0:1, :], q11, new1))
        body = jnp.where(at0 | at1, 0.0, work) - col0 * new0 - col1 * new1
        work = jnp.where(row == k, new0, jnp.where(row == k + 1, new1, body))
    inv_out, inv_in = work[:, 0:64], work[:, 64:128]
    zero = jnp.zeros((64, 64), F32)
    twice = jnp.concatenate(
        [jnp.concatenate([inv_in, zero], axis=1), jnp.concatenate([zero, inv_in], axis=1)], axis=0
    )
    pairs = []
    for grams in (mine, theirs):
        for d in range(0, count, 2):
            pairs.append(jnp.concatenate([grams[d, 0:64, 64:128], grams[d + 1, 0:64, 64:128]], axis=1))
    half = split_dot(jnp.concatenate(pairs, axis=0), twice)
    half = jnp.concatenate([half[64 * p : 64 * p + 64, :] for p in range(len(pairs))], axis=1)
    white = split_dot(inv_out, half)
    core = place_ref[3]
    for at in range(2 * count):
        d = at % count
        owner = core if at < count else 1 - core
        seq = (d % NY * NC + owner) * NX + d // NY
        out[seq] = white[:, 64 * at : 64 * at + 64].astype(BF16)


def full(shape, dtype=F32):
    return jax.ShapeDtypeStruct(shape, dtype)


VMEM = pl.BlockSpec(memory_space=pltpu.VMEM)
SMEM = pl.BlockSpec(memory_space=pltpu.SMEM)
ANY = pl.BlockSpec(memory_space=pl.ANY)
ZAXIS = ("zh", "zl")


def per_device(hidden, head_weight, in_proj, out_proj, targets, lengths, grad_store):
    token_count, width = hidden.shape
    x = lax.axis_index("x")
    z = lax.axis_index("zh") * ZL + lax.axis_index("zl")
    core = lax.axis_index("c")
    rows = lax.axis_index("y") * NC + core
    place = jnp.stack([x, z, rows * NX + x, core]).astype(jnp.int32)
    cols = head_weight.shape[1]
    head = lax.all_gather(head_weight, ("y", "c"), axis=0, tiled=True)
    picked, in_rows, out_rows = pl.pallas_call(
        prepare_kernel,
        out_shape=(full((token_count, 64)), full(in_proj.shape, BF16), full(out_proj.shape, BF16)),
        in_specs=[SMEM, VMEM, VMEM, VMEM],
        out_specs=(VMEM, VMEM, VMEM),
        name="prepare",
    )(place, in_proj, out_proj, targets[:, None])
    strided = spread(hidden.T, "zh", ZH)
    strided, picked, in_rows, out_rows = lax.optimization_barrier((strided, picked, in_rows, out_rows))
    size = NX * ZH * HALF
    a_own = strided[:, :HALF, :].reshape(ZH * HALF, token_count).T
    a_parts = [a_own] + [shift(a_own, ZAXIS, -s, NZ) for s in STEPS[1:]]
    b_own = spread(strided[:, HALF:, :].reshape(ZH * HALF, token_count), "x", NX)
    b_own = b_own.reshape(size, token_count).T
    a_own = jnp.concatenate(a_parts, axis=1)
    b_back, b_next = shift(b_own, ZAXIS, 1, NZ), shift(b_own, ZAXIS, -1, NZ)
    a_back, a_next = shift(a_own, "x", 1, NX), shift(a_own, "x", -1, NX)
    b_far, a_far = shift(b_back, ZAXIS, 1, NZ), shift(a_back, "x", 1, NX)
    chunks = [a_own, a_back, a_next, a_far, b_own, b_back, b_next, b_far]
    head = head.reshape(NX, ZH, ZL, 2, HALF, cols)
    in_rows = in_rows.reshape(NX, ZH, ZL, 2, HALF, 64)

    def buffers(count):
        return [
            pltpu.VMEM((count, token_count, size), BF16),
            pltpu.VMEM((count, NX, ZH, HALF, cols), BF16),
            pltpu.VMEM((count, NX, ZH, HALF, 64), BF16),
            pltpu.SemaphoreType.DMA((count, 1 + 2 * ZL)),
            pltpu.VMEM((token_count, cols), F32),
        ]

    acc, proj = pl.pallas_call(
        first_kernel,
        out_shape=(full((token_count, cols)), full((TILE, 64))),
        in_specs=[SMEM] + [ANY] * (len(EARLY) + 2),
        out_specs=(ANY, VMEM),
        scratch_shapes=buffers(len(EARLY)) + [pltpu.SemaphoreType.DMA((cols // BLOCK,))],
        name="logits_first",
    )(place, *[chunks[j] for j in EARLY], head, in_rows)
    packed, proj = pl.pallas_call(
        logits_kernel,
        out_shape=(full((NX * ZL, ROWS + 8, TILE)), full((TILE, 64))),
        in_specs=[SMEM] + [ANY] * (len(LATE) + 3) + [VMEM] * 3,
        out_specs=(VMEM, VMEM),
        scratch_shapes=buffers(len(LATE)) + [pltpu.SemaphoreType.DMA(())],
        name="logits_last",
    )(place, *[chunks[j] for j in LATE], head, in_rows, acc, proj, out_rows, picked)
    merged = pl.pallas_call(
        merge_kernel,
        out_shape=full((NZ, ROWS + 8, TILE)),
        in_specs=[SMEM, VMEM],
        out_specs=VMEM,
        scratch_shapes=[pltpu.VMEM((TILE, TILE), F32)],
        name="merge",
    )(place, exchange(packed, ("x", "zl")))
    seqs = NX * NY * NC
    gram = pl.pallas_call(
        gram_kernel,
        out_shape=full((NX * NY, 72, TILE)),
        in_specs=[SMEM, SMEM, VMEM, VMEM],
        out_specs=VMEM,
        name="gram",
    )(place, lengths, exchange(merged, ZAXIS), proj)
    mine = exchange(gram, ("x", "y"))
    theirs = lax.ppermute(mine, "c", [(0, 1), (1, 0)])
    whitened = pl.pallas_call(
        whiten_kernel,
        out_shape=full((seqs, 64, 64), BF16),
        in_specs=[SMEM, SMEM, VMEM, VMEM],
        out_specs=VMEM,
        name="whiten",
    )(place, lengths, mine, theirs)
    whitened = whitened.reshape(seqs, 64 * 64)
    return jnp.dot(whitened, grad_store.T, preferred_element_type=F32)


def solution(mesh):
    grid = Mesh(mesh.devices.reshape(NX, ZH, ZL, NY, NC), ("x", "zh", "zl", "y", "c"))
    return jax.shard_map(
        per_device,
        mesh=grid,
        in_specs=(
            P(("y", "c"), ("x", "zh", "zl")),
            P(("y", "c"), ("x", "zh", "zl")),
            P(),
            P(("x", "zh", "zl"), None),
            P(("y", "c")),
            P(),
            P(("x", "zh", "zl", "y", "c"), None),
        ),
        out_specs=P(None, ("x", "zh", "zl", "y", "c")),
        check_vma=False,
    )
```

```python
import functools
import jax
import jax.numpy as jnp
from jax import lax
from jax.experimental import pallas as pl
from jax.experimental.pallas import tpu as pltpu
from jax.sharding import Mesh, PartitionSpec as P

TILE = 128
NX, NZ, NY, NC = 4, 16, 4, 2
ZH, ZL = 4, 4
HALF = 32
ROWS = TILE // ZL
STEPS = (0, -1, 1, -2)
BLOCK = 1024
UNROLL = 4
EARLY, LATE = (0, 4, 1, 2, 5, 6), (3, 7)

damping_ratio = 0.1
tiny_value = 1e-06
HI = lax.Precision.HIGHEST
F32 = jnp.float32
BF16 = jnp.bfloat16


def shift(value, axis, step, size):
    return lax.ppermute(value, axis, [(i, (i + step) % size) for i in range(size)])


def spread(value, axis, size):
    copies = jnp.broadcast_to(value[None], (size,) + value.shape)
    return lax.all_to_all(copies, axis, 0, 0, tiled=True)


def exchange(value, axis):
    return lax.all_to_all(value, axis, 0, 0, tiled=True)


def prepare_kernel(place_ref, in_proj, out_proj, targets, picked, in_copy, out_copy):
    x, z = place_ref[0], place_ref[1]
    table = out_proj[...]
    cols = table.shape[0]
    column = lax.broadcasted_iota(jnp.int32, (targets.shape[0], cols), 1) + (x * NZ + z) * cols
    hit = jnp.where(column == targets[...], 1.0, 0.0).astype(BF16)
    picked[...] = jnp.dot(hit, table, preferred_element_type=F32)
    in_copy[...] = in_proj[...]
    out_copy[...] = table


def stat_tile(peak, total, rows):
    lane = lax.broadcasted_iota(jnp.int32, (rows, TILE), 1)
    stat = jnp.where(lane == 0, peak, jnp.where(lane == 1, total, 0.0))
    if rows < TILE:
        stat = jnp.concatenate([stat, jnp.zeros((TILE - rows, TILE), F32)], axis=0)
    return stat.T[0:8, :]


def fetch(js, chunks, head, in_proj, x, z, feat_buf, head_buf, proj_buf, sems):
    waits, late_waits = [], []
    for at, j in enumerate(js):
        step = STEPS[j % len(STEPS)]
        copies = [pltpu.make_async_copy(chunks[at], feat_buf.at[at], sems.at[at, 0])]
        others = []
        for a in range(4):
            if j < len(STEPS):
                xs, zs, half = (x + step + NX) % NX, a, 0
            else:
                xs, zs, half = (x + STEPS[a] + NX) % NX, (z + step + NZ) % ZL, 1
            copies.append(pltpu.make_async_copy(head.at[xs, :, zs, half], head_buf.at[at, a], sems.at[at, 1 + a]))
            others.append(pltpu.make_async_copy(in_proj.at[xs, :, zs, half], proj_buf.at[at, a], sems.at[at, 5 + a]))
        for copy in copies:
            copy.start()
        waits.append(copies)
        late_waits += others
    for copy in late_waits:
        copy.start()
    return waits, late_waits


def add_products(waits, feat_buf, head_buf, out, ready=None, then=None):
    count, width = feat_buf.shape[0], feat_buf.shape[2]
    for g in range(0, count, 2):
        for copy in waits[g] + waits[g + 1]:
            copy.wait()
        if g == 0 and ready is not None:
            ready.wait()

        def column_block(n, carry, g=g):
            at = pl.ds(pl.multiple_of(n * BLOCK, BLOCK), BLOCK)
            part = None if g == 0 and ready is None else out[:, at]
            for j in (g, g + 1):
                more = jnp.dot(feat_buf[j], head_buf[j, :, :, :, at].reshape(width, BLOCK), preferred_element_type=F32)
                part = more if part is None else part + more
            out[:, at] = part
            if then is not None and g + 2 == count:
                then(n, at).start()
            return carry

        lax.fori_loop(0, out.shape[1] // BLOCK, column_block, 0)


def project(feat_buf, proj_buf, x, waits):
    own = pl.ds(pl.multiple_of(x * TILE, TILE), TILE)
    for copy in waits:
        copy.wait()
    return sum(
        jnp.dot(feat_buf[j, own, :], proj_buf[j].reshape(feat_buf.shape[2], 64), preferred_element_type=F32)
        for j in range(feat_buf.shape[0])
    )


def first_kernel(place_ref, *refs):
    chunks = refs[: len(EARLY)]
    head, in_proj, acc, proj, feat_buf, head_buf, proj_buf, sems, acc_buf, out_sems = refs[len(EARLY) :]
    x, z = place_ref[0], place_ref[1]
    waits, others = fetch(EARLY, chunks, head, in_proj, x, z, feat_buf, head_buf, proj_buf, sems)

    def store(n, at):
        return pltpu.make_async_copy(acc_buf.at[:, at], acc.at[:, at], out_sems.at[n])

    add_products(waits, feat_buf, head_buf, acc_buf, then=store)
    proj[...] = project(feat_buf, proj_buf, x, others)
    for n in range(acc_buf.shape[1] // BLOCK):
        store(n, pl.ds(n * BLOCK, BLOCK)).wait()


def logits_kernel(place_ref, *refs):
    chunks = refs[: len(LATE)]
    head, in_proj, acc, proj_in, out_proj, picked, packed, proj = refs[len(LATE) : len(LATE) + 8]
    feat_buf, head_buf, proj_buf, sems, logit_buf, in_sem = refs[len(LATE) + 8 :]
    x, z = place_ref[0], place_ref[1]
    waits, others = fetch(LATE, chunks, head, in_proj, x, z, feat_buf, head_buf, proj_buf, sems)
    ready = pltpu.make_async_copy(acc, logit_buf, in_sem)
    ready.start()
    add_products(waits, feat_buf, head_buf, logit_buf, ready=ready)
    proj[...] = proj_in[...] + project(feat_buf, proj_buf, x, others)
    table = out_proj[...]

    def row_block(i, carry):
        rows = pl.ds(pl.multiple_of(i * TILE, TILE), TILE)
        logits = logit_buf[rows, :]
        peak = jnp.max(logits, axis=1, keepdims=True)
        weight = jnp.exp(logits - peak)
        total = jnp.sum(weight, axis=1, keepdims=True)
        part1 = weight.astype(BF16)
        rest = weight - part1.astype(F32)
        part2 = rest.astype(BF16)
        part3 = (rest - part2.astype(F32)).astype(BF16)
        mixed = jnp.dot(part1, table, preferred_element_type=F32)
        mixed += jnp.dot(part2, table, preferred_element_type=F32)
        mixed += jnp.dot(part3, table, preferred_element_type=F32)
        data = jnp.concatenate([mixed, picked[rows, :]], axis=1)
        stat = stat_tile(peak, total, TILE)
        for b in range(ZL):
            packed[i * ZL + b, 0:ROWS, :] = data[b * ROWS : (b + 1) * ROWS, :]
            packed[i * ZL + b, ROWS : ROWS + 8, :] = stat
        return carry

    lax.fori_loop(0, NX, row_block, 0, unroll=UNROLL)


def merge(parts):
    peak = functools.reduce(jnp.maximum, [p for _, p, _ in parts])
    scales = [jnp.exp(p - peak) for _, p, _ in parts]
    total = sum(s * t for s, (_, _, t) in zip(scales, parts))
    mixed = sum(s * data[:, :64] for s, (data, _, _) in zip(scales, parts))
    picked = sum(data[:, 64:] for data, _, _ in parts)
    return mixed, picked, peak, total


def merge_kernel(place_ref, packed, out, turned):
    low = place_ref[1] % ZL
    count = packed.shape[0]
    turned[...] = packed[:, ROWS : ROWS + 8, :].reshape(count * 8, TILE).T
    stat = turned[pl.ds(pl.multiple_of(low * ROWS, ROWS), ROWS), :]
    parts = [(packed[i, 0:ROWS, :], stat[:, 8 * i : 8 * i + 1], stat[:, 8 * i + 1 : 8 * i + 2]) for i in range(count)]
    mixed, picked, peak, total = merge(parts)
    data, stat = jnp.concatenate([mixed, picked], axis=1), stat_tile(peak, total, ROWS)
    for i in range(NZ):
        out[i, 0:ROWS, :] = data
        out[i, ROWS : ROWS + 8, :] = stat


def gram_kernel(place_ref, lengths, packed, proj, out):
    stat = packed[:, ROWS : ROWS + 8, :].reshape(NZ * 8, TILE).T[0:ROWS, :]
    blocks = []
    for b in range(ZL):
        parts = []
        for i in range(ZH):
            at = i * ZL + b
            parts.append((packed[at, 0:ROWS, :], stat[:, 8 * at : 8 * at + 1], stat[:, 8 * at + 1 : 8 * at + 2]))
        mixed, picked, _, total = merge(parts)
        blocks.append(mixed / total - picked)
    length = lengths[place_ref[2]]
    both = jnp.concatenate([jnp.concatenate(blocks, axis=0), proj[...]], axis=1)
    row = lax.broadcasted_iota(jnp.int32, both.shape, 0)
    both = jnp.where(row < length, both, 0.0)
    gram = lax.dot_general(both, both, (((0,), (0,)), ((), ())), precision=HI, preferred_element_type=F32)
    row = lax.broadcasted_iota(jnp.int32, (64, 64), 0)
    col = lax.broadcasted_iota(jnp.int32, (64, 64), 1)
    cov_in = gram[64:128, 64:128]
    root = jnp.sqrt(jnp.full((64, 64), length.astype(F32)))
    data = jnp.concatenate([jnp.where(row <= col, gram[0:64, 0:64], cov_in), gram[0:64, 64:128] / root], axis=1)
    diag = jnp.sum(jnp.where(row == col, cov_in, 0.0), axis=0, keepdims=True)
    diag = jnp.broadcast_to(jnp.concatenate([diag, diag], axis=1), (8, TILE))
    for i in range(out.shape[0]):
        out[i, 0:64, :] = data
        out[i, 64:72, :] = diag


def split_dot(a, b):
    a_top, b_top = a.astype(BF16), b.astype(BF16)
    a_rest, b_rest = (a - a_top.astype(F32)).astype(BF16), (b - b_top.astype(F32)).astype(BF16)
    out = jnp.dot(a_top, b_top, preferred_element_type=F32)
    out += jnp.dot(a_top, b_rest, preferred_element_type=F32)
    return out + jnp.dot(a_rest, b_top, preferred_element_type=F32)


def whiten_kernel(place_ref, lengths, mine, theirs, out):
    total = functools.reduce(jnp.add, [lengths[s] for s in range(lengths.shape[0])]).astype(F32)
    count = mine.shape[0]
    summed = functools.reduce(jnp.add, [mine[d] for d in range(count)])
    summed = (summed + functools.reduce(jnp.add, [theirs[d] for d in range(count)])) / total
    row = lax.broadcasted_iota(jnp.int32, (64, TILE), 0)
    lane = lax.broadcasted_iota(jnp.int32, (64, TILE), 1)
    left = lane < 64
    inner = jnp.where(left, lane, lane - 64)
    block = jnp.where(left, summed[0:64, :], 0.0)
    turned = jnp.concatenate([block, jnp.zeros_like(block)], axis=0).T[0:64, :]
    upper, lower = row < inner, row > inner
    cov_out = jnp.where(lower, turned, block)[:, 0:64]
    cov_in = jnp.where(upper, turned, block)[:, 0:64]
    work = jnp.concatenate([cov_out, cov_in], axis=1)
    on_diag = row == inner
    work = jnp.where(on_diag & (lane >= 64), summed[64:65, :], work)
    diag = jnp.where(on_diag, work, 0.0)
    trace_out = jnp.sum(jnp.where(left, diag, 0.0))
    trace_in = jnp.sum(jnp.where(left, 0.0, diag))
    damp = jnp.where(left, damping_ratio * trace_out / 64 + tiny_value, damping_ratio * trace_in / 64 + tiny_value)
    work = work + jnp.where(on_diag, damp, 0.0)
    def column(work, k):
        return jnp.where(left, work[:, k : k + 1], work[:, 64 + k : 65 + k])

    for k in range(0, 64, 2):
        at0, at1 = inner == k, inner == k + 1
        row0, row1 = work[k : k + 1, :], work[k + 1 : k + 2, :]
        col0, col1 = column(work, k), column(work, k + 1)
        p00, p01 = col0[k : k + 1, :], col1[k : k + 1, :]
        p10, p11 = col0[k + 1 : k + 2, :], col1[k + 1 : k + 2, :]
        inv = 1.0 / (p00 * p11 - p01 * p10)
        q00, q01, q10, q11 = p11 * inv, -p01 * inv, -p10 * inv, p00 * inv
        new0, new1 = q00 * row0 + q01 * row1, q10 * row0 + q11 * row1
        new0 = jnp.where(at0[0:1, :], q00, jnp.where(at1[0:1, :], q01, new0))
        new1 = jnp.where(at0[0:1, :], q10, jnp.where(at1[0:1, :], q11, new1))
        body = jnp.where(at0 | at1, 0.0, work) - col0 * new0 - col1 * new1
        work = jnp.where(row == k, new0, jnp.where(row == k + 1, new1, body))
    inv_out, inv_in = work[:, 0:64], work[:, 64:128]
    zero = jnp.zeros((64, 64), F32)
    twice = jnp.concatenate(
        [jnp.concatenate([inv_in, zero], axis=1), jnp.concatenate([zero, inv_in], axis=1)], axis=0
    )
    pairs = []
    for grams in (mine, theirs):
        for d in range(0, count, 2):
            pairs.append(jnp.concatenate([grams[d, 0:64, 64:128], grams[d + 1, 0:64, 64:128]], axis=1))
    half = split_dot(jnp.concatenate(pairs, axis=0), twice)
    half = jnp.concatenate([half[64 * p : 64 * p + 64, :] for p in range(len(pairs))], axis=1)
    white = split_dot(inv_out, half)
    core = place_ref[3]
    for at in range(2 * count):
        d = at % count
        owner = core if at < count else 1 - core
        seq = (d % NY * NC + owner) * NX + d // NY
        out[seq] = white[:, 64 * at : 64 * at + 64].astype(BF16)


def full(shape, dtype=F32):
    return jax.ShapeDtypeStruct(shape, dtype)


VMEM = pl.BlockSpec(memory_space=pltpu.VMEM)
SMEM = pl.BlockSpec(memory_space=pltpu.SMEM)
ANY = pl.BlockSpec(memory_space=pl.ANY)
ZAXIS = ("zh", "zl")


def per_device(hidden, head_weight, in_proj, out_proj, targets, lengths, grad_store):
    token_count, width = hidden.shape
    x = lax.axis_index("x")
    z = lax.axis_index("zh") * ZL + lax.axis_index("zl")
    core = lax.axis_index("c")
    rows = lax.axis_index("y") * NC + core
    place = jnp.stack([x, z, rows * NX + x, core]).astype(jnp.int32)
    cols = head_weight.shape[1]
    head = lax.all_gather(head_weight, ("y", "c"), axis=0, tiled=True)
    picked, in_rows, out_rows = pl.pallas_call(
        prepare_kernel,
        out_shape=(full((token_count, 64)), full(in_proj.shape, BF16), full(out_proj.shape, BF16)),
        in_specs=[SMEM, VMEM, VMEM, VMEM],
        out_specs=(VMEM, VMEM, VMEM),
        name="prepare",
    )(place, in_proj, out_proj, targets[:, None])
    strided = spread(hidden.T, "zh", ZH)
    strided, picked, in_rows, out_rows = lax.optimization_barrier((strided, picked, in_rows, out_rows))
    size = NX * ZH * HALF
    a_own = spread(strided[:, :HALF, :].reshape(ZH * HALF, token_count), "zl", ZL)
    a_own = a_own.reshape(size, token_count).T
    b_part = strided[:, HALF:, :].reshape(ZH * HALF, token_count).T
    b_own = jnp.concatenate([b_part] + [shift(b_part, "x", -s, NX) for s in STEPS[1:]], axis=1)
    b_back, b_next = shift(b_own, ZAXIS, 1, NZ), shift(b_own, ZAXIS, -1, NZ)
    a_back, a_next = shift(a_own, "x", 1, NX), shift(a_own, "x", -1, NX)
    b_far, a_far = shift(b_back, ZAXIS, 1, NZ), shift(a_back, "x", 1, NX)
    chunks = [a_own, a_back, a_next, a_far, b_own, b_back, b_next, b_far]
    head = head.reshape(NX, ZH, ZL, 2, HALF, cols)
    in_rows = in_rows.reshape(NX, ZH, ZL, 2, HALF, 64)

    def buffers(count):
        return [
            pltpu.VMEM((count, token_count, size), BF16),
            pltpu.VMEM((count, NX, ZH, HALF, cols), BF16),
            pltpu.VMEM((count, NX, ZH, HALF, 64), BF16),
            pltpu.SemaphoreType.DMA((count, 1 + 2 * ZL)),
            pltpu.VMEM((token_count, cols), F32),
        ]

    acc, proj = pl.pallas_call(
        first_kernel,
        out_shape=(full((token_count, cols)), full((TILE, 64))),
        in_specs=[SMEM] + [ANY] * (len(EARLY) + 2),
        out_specs=(ANY, VMEM),
        scratch_shapes=buffers(len(EARLY)) + [pltpu.SemaphoreType.DMA((cols // BLOCK,))],
        name="logits_first",
    )(place, *[chunks[j] for j in EARLY], head, in_rows)
    packed, proj = pl.pallas_call(
        logits_kernel,
        out_shape=(full((NX * ZL, ROWS + 8, TILE)), full((TILE, 64))),
        in_specs=[SMEM] + [ANY] * (len(LATE) + 3) + [VMEM] * 3,
        out_specs=(VMEM, VMEM),
        scratch_shapes=buffers(len(LATE)) + [pltpu.SemaphoreType.DMA(())],
        name="logits_last",
    )(place, *[chunks[j] for j in LATE], head, in_rows, acc, proj, out_rows, picked)
    merged = pl.pallas_call(
        merge_kernel,
        out_shape=full((NZ, ROWS + 8, TILE)),
        in_specs=[SMEM, VMEM],
        out_specs=VMEM,
        scratch_shapes=[pltpu.VMEM((TILE, TILE), F32)],
        name="merge",
    )(place, exchange(packed, ("x", "zl")))
    seqs = NX * NY * NC
    gram = pl.pallas_call(
        gram_kernel,
        out_shape=full((NX * NY, 72, TILE)),
        in_specs=[SMEM, SMEM, VMEM, VMEM],
        out_specs=VMEM,
        name="gram",
    )(place, lengths, exchange(merged, ZAXIS), proj)
    mine = exchange(gram, ("x", "y"))
    theirs = lax.ppermute(mine, "c", [(0, 1), (1, 0)])
    whitened = pl.pallas_call(
        whiten_kernel,
        out_shape=full((seqs, 64, 64), BF16),
        in_specs=[SMEM, SMEM, VMEM, VMEM],
        out_specs=VMEM,
        name="whiten",
    )(place, lengths, mine, theirs)
    whitened = whitened.reshape(seqs, 64 * 64)
    return jnp.dot(whitened, grad_store.T, preferred_element_type=F32)


def solution(mesh):
    grid = Mesh(mesh.devices.reshape(NX, ZH, ZL, NY, NC), ("x", "zh", "zl", "y", "c"))
    return jax.shard_map(
        per_device,
        mesh=grid,
        in_specs=(
            P(("y", "c"), ("x", "zh", "zl")),
            P(("y", "c"), ("x", "zh", "zl")),
            P(),
            P(("x", "zh", "zl"), None),
            P(("y", "c")),
            P(),
            P(("x", "zh", "zl", "y", "c"), None),
        ),
        out_specs=P(None, ("x", "zh", "zl", "y", "c")),
        check_vma=False,
    )
```

```python
import functools
import jax
import jax.numpy as jnp
from jax import lax
from jax.experimental import pallas as pl
from jax.experimental.pallas import tpu as pltpu
from jax.sharding import Mesh, PartitionSpec as P

TILE = 128
NX, NZ, NY, NC = 4, 16, 4, 2
ZH, ZL = 4, 4
HALF = 32
ROWS = TILE // ZL
STEPS = (0, -1, 1, -2)
BLOCK = 1024
UNROLL = 4
EARLY, LATE = (0, 4, 1, 2, 5, 6), (3, 7)

damping_ratio = 0.1
tiny_value = 1e-06
HI = lax.Precision.HIGHEST
F32 = jnp.float32
BF16 = jnp.bfloat16


def shift(value, axis, step, size):
    return lax.ppermute(value, axis, [(i, (i + step) % size) for i in range(size)])


def spread(value, axis, size):
    copies = jnp.broadcast_to(value[None], (size,) + value.shape)
    return lax.all_to_all(copies, axis, 0, 0, tiled=True)


def exchange(value, axis):
    return lax.all_to_all(value, axis, 0, 0, tiled=True)


def prepare_kernel(place_ref, in_proj, out_proj, targets, picked, in_copy, out_copy):
    x, z = place_ref[0], place_ref[1]
    table = out_proj[...]
    cols = table.shape[0]
    column = lax.broadcasted_iota(jnp.int32, (targets.shape[0], cols), 1) + (x * NZ + z) * cols
    hit = jnp.where(column == targets[...], 1.0, 0.0).astype(BF16)
    picked[...] = jnp.dot(hit, table, preferred_element_type=F32)
    in_copy[...] = in_proj[...]
    out_copy[...] = table


def stat_tile(peak, total, rows):
    lane = lax.broadcasted_iota(jnp.int32, (rows, TILE), 1)
    stat = jnp.where(lane == 0, peak, jnp.where(lane == 1, total, 0.0))
    if rows < TILE:
        stat = jnp.concatenate([stat, jnp.zeros((TILE - rows, TILE), F32)], axis=0)
    return stat.T[0:8, :]


def fetch(js, chunks, head, in_proj, x, z, feat_buf, head_buf, proj_buf, sems):
    waits, late_waits = [], []
    for at, j in enumerate(js):
        step = STEPS[j % len(STEPS)]
        copies = [pltpu.make_async_copy(chunks[at], feat_buf.at[at], sems.at[at, 0])]
        others = []
        for a in range(4):
            if j < len(STEPS):
                xs, zs, half = (x + step + NX) % NX, a, 0
            else:
                xs, zs, half = (x + STEPS[a] + NX) % NX, (z + step + NZ) % ZL, 1
            copies.append(pltpu.make_async_copy(head.at[xs, :, zs, half], head_buf.at[at, a], sems.at[at, 1 + a]))
            others.append(pltpu.make_async_copy(in_proj.at[xs, :, zs, half], proj_buf.at[at, a], sems.at[at, 5 + a]))
        for copy in copies:
            copy.start()
        waits.append(copies)
        late_waits += others
    for copy in late_waits:
        copy.start()
    return waits, late_waits


def add_products(waits, feat_buf, head_buf, out, ready=None, then=None):
    count, width = feat_buf.shape[0], feat_buf.shape[2]
    for g in range(0, count, 2):
        for copy in waits[g] + waits[g + 1]:
            copy.wait()
        if g == 0 and ready is not None:
            ready.wait()

        def column_block(n, carry, g=g):
            at = pl.ds(pl.multiple_of(n * BLOCK, BLOCK), BLOCK)
            part = None if g == 0 and ready is None else out[:, at]
            for j in (g, g + 1):
                more = jnp.dot(feat_buf[j], head_buf[j, :, :, :, at].reshape(width, BLOCK), preferred_element_type=F32)
                part = more if part is None else part + more
            out[:, at] = part
            if then is not None and g + 2 == count:
                then(n, at).start()
            return carry

        lax.fori_loop(0, out.shape[1] // BLOCK, column_block, 0)


def project(feat_buf, proj_buf, x, waits):
    own = pl.ds(pl.multiple_of(x * TILE, TILE), TILE)
    for copy in waits:
        copy.wait()
    return sum(
        jnp.dot(feat_buf[j, own, :], proj_buf[j].reshape(feat_buf.shape[2], 64), preferred_element_type=F32)
        for j in range(feat_buf.shape[0])
    )


def first_kernel(place_ref, *refs):
    chunks = refs[: len(EARLY)]
    head, in_proj, acc, proj, feat_buf, head_buf, proj_buf, sems, acc_buf, out_sems = refs[len(EARLY) :]
    x, z = place_ref[0], place_ref[1]
    waits, others = fetch(EARLY, chunks, head, in_proj, x, z, feat_buf, head_buf, proj_buf, sems)

    def store(n, at):
        return pltpu.make_async_copy(acc_buf.at[:, at], acc.at[:, at], out_sems.at[n])

    add_products(waits, feat_buf, head_buf, acc_buf, then=store)
    proj[...] = project(feat_buf, proj_buf, x, others)
    for n in range(acc_buf.shape[1] // BLOCK):
        store(n, pl.ds(n * BLOCK, BLOCK)).wait()


def logits_kernel(place_ref, *refs):
    chunks = refs[: len(LATE)]
    head, in_proj, acc, proj_in, out_proj, picked, packed, proj = refs[len(LATE) : len(LATE) + 8]
    feat_buf, head_buf, proj_buf, sems, logit_buf, in_sem = refs[len(LATE) + 8 :]
    x, z = place_ref[0], place_ref[1]
    waits, others = fetch(LATE, chunks, head, in_proj, x, z, feat_buf, head_buf, proj_buf, sems)
    ready = pltpu.make_async_copy(acc, logit_buf, in_sem)
    ready.start()
    add_products(waits, feat_buf, head_buf, logit_buf, ready=ready)
    proj[...] = proj_in[...] + project(feat_buf, proj_buf, x, others)
    table = out_proj[...]

    def row_block(i, carry):
        rows = pl.ds(pl.multiple_of(i * TILE, TILE), TILE)
        logits = logit_buf[rows, :]
        peak = jnp.max(logits, axis=1, keepdims=True)
        weight = jnp.exp(logits - peak)
        total = jnp.sum(weight, axis=1, keepdims=True)
        part1 = weight.astype(BF16)
        rest = weight - part1.astype(F32)
        part2 = rest.astype(BF16)
        part3 = (rest - part2.astype(F32)).astype(BF16)
        parts = jnp.dot(jnp.concatenate([part1, part2, part3], axis=0), table, preferred_element_type=F32)
        mixed = parts[0:TILE] + parts[TILE : 2 * TILE] + parts[2 * TILE :]
        data = jnp.concatenate([mixed, picked[rows, :]], axis=1)
        stat = stat_tile(peak, total, TILE)
        for b in range(ZL):
            packed[i * ZL + b, 0:ROWS, :] = data[b * ROWS : (b + 1) * ROWS, :]
            packed[i * ZL + b, ROWS : ROWS + 8, :] = stat
        return carry

    lax.fori_loop(0, NX, row_block, 0, unroll=UNROLL)


def merge(parts):
    peak = functools.reduce(jnp.maximum, [p for _, p, _ in parts])
    scales = [jnp.exp(p - peak) for _, p, _ in parts]
    total = sum(s * t for s, (_, _, t) in zip(scales, parts))
    mixed = sum(s * data[:, :64] for s, (data, _, _) in zip(scales, parts))
    picked = sum(data[:, 64:] for data, _, _ in parts)
    return mixed, picked, peak, total


def merge_kernel(place_ref, packed, out, turned):
    low = place_ref[1] % ZL
    count = packed.shape[0]
    turned[...] = packed[:, ROWS : ROWS + 8, :].reshape(count * 8, TILE).T
    stat = turned[pl.ds(pl.multiple_of(low * ROWS, ROWS), ROWS), :]
    parts = [(packed[i, 0:ROWS, :], stat[:, 8 * i : 8 * i + 1], stat[:, 8 * i + 1 : 8 * i + 2]) for i in range(count)]
    mixed, picked, peak, total = merge(parts)
    data, stat = jnp.concatenate([mixed, picked], axis=1), stat_tile(peak, total, ROWS)
    for i in range(NZ):
        out[i, 0:ROWS, :] = data
        out[i, ROWS : ROWS + 8, :] = stat


def gram_kernel(place_ref, lengths, packed, proj, out):
    stat = packed[:, ROWS : ROWS + 8, :].reshape(NZ * 8, TILE).T[0:ROWS, :]
    blocks = []
    for b in range(ZL):
        parts = []
        for i in range(ZH):
            at = i * ZL + b
            parts.append((packed[at, 0:ROWS, :], stat[:, 8 * at : 8 * at + 1], stat[:, 8 * at + 1 : 8 * at + 2]))
        mixed, picked, _, total = merge(parts)
        blocks.append(mixed / total - picked)
    length = lengths[place_ref[2]]
    both = jnp.concatenate([jnp.concatenate(blocks, axis=0), proj[...]], axis=1)
    row = lax.broadcasted_iota(jnp.int32, both.shape, 0)
    both = jnp.where(row < length, both, 0.0)
    gram = lax.dot_general(both, both, (((0,), (0,)), ((), ())), precision=HI, preferred_element_type=F32)
    row = lax.broadcasted_iota(jnp.int32, (64, 64), 0)
    col = lax.broadcasted_iota(jnp.int32, (64, 64), 1)
    cov_in = gram[64:128, 64:128]
    root = jnp.sqrt(jnp.full((64, 64), length.astype(F32)))
    data = jnp.concatenate([jnp.where(row <= col, gram[0:64, 0:64], cov_in), gram[0:64, 64:128] / root], axis=1)
    diag = jnp.sum(jnp.where(row == col, cov_in, 0.0), axis=0, keepdims=True)
    diag = jnp.broadcast_to(jnp.concatenate([diag, diag], axis=1), (8, TILE))
    for i in range(out.shape[0]):
        out[i, 0:64, :] = data
        out[i, 64:72, :] = diag


def split_dot(a, b):
    a_top, b_top = a.astype(BF16), b.astype(BF16)
    a_rest, b_rest = (a - a_top.astype(F32)).astype(BF16), (b - b_top.astype(F32)).astype(BF16)
    out = jnp.dot(a_top, b_top, preferred_element_type=F32)
    out += jnp.dot(a_top, b_rest, preferred_element_type=F32)
    return out + jnp.dot(a_rest, b_top, preferred_element_type=F32)


def whiten_kernel(place_ref, lengths, mine, theirs, out):
    total = functools.reduce(jnp.add, [lengths[s] for s in range(lengths.shape[0])]).astype(F32)
    count = mine.shape[0]
    summed = functools.reduce(jnp.add, [mine[d] for d in range(count)])
    summed = (summed + functools.reduce(jnp.add, [theirs[d] for d in range(count)])) / total
    row = lax.broadcasted_iota(jnp.int32, (64, TILE), 0)
    lane = lax.broadcasted_iota(jnp.int32, (64, TILE), 1)
    left = lane < 64
    inner = jnp.where(left, lane, lane - 64)
    block = jnp.where(left, summed[0:64, :], 0.0)
    turned = jnp.concatenate([block, jnp.zeros_like(block)], axis=0).T[0:64, :]
    upper, lower = row < inner, row > inner
    cov_out = jnp.where(lower, turned, block)[:, 0:64]
    cov_in = jnp.where(upper, turned, block)[:, 0:64]
    work = jnp.concatenate([cov_out, cov_in], axis=1)
    on_diag = row == inner
    work = jnp.where(on_diag & (lane >= 64), summed[64:65, :], work)
    diag = jnp.where(on_diag, work, 0.0)
    trace_out = jnp.sum(jnp.where(left, diag, 0.0))
    trace_in = jnp.sum(jnp.where(left, 0.0, diag))
    damp = jnp.where(left, damping_ratio * trace_out / 64 + tiny_value, damping_ratio * trace_in / 64 + tiny_value)
    work = work + jnp.where(on_diag, damp, 0.0)

    def column(work, k):
        return jnp.where(left, work[:, k : k + 1], work[:, 64 + k : 65 + k])

    for k in range(0, 64, 2):
        at0, at1 = inner == k, inner == k + 1
        row0, row1 = work[k : k + 1, :], work[k + 1 : k + 2, :]
        col0, col1 = column(work, k), column(work, k + 1)
        p00, p01 = col0[k : k + 1, :], col1[k : k + 1, :]
        p10, p11 = col0[k + 1 : k + 2, :], col1[k + 1 : k + 2, :]
        inv = 1.0 / (p00 * p11 - p01 * p10)
        q00, q01, q10, q11 = p11 * inv, -p01 * inv, -p10 * inv, p00 * inv
        new0, new1 = q00 * row0 + q01 * row1, q10 * row0 + q11 * row1
        new0 = jnp.where(at0[0:1, :], q00, jnp.where(at1[0:1, :], q01, new0))
        new1 = jnp.where(at0[0:1, :], q10, jnp.where(at1[0:1, :], q11, new1))
        body = jnp.where(at0 | at1, 0.0, work) - col0 * new0 - col1 * new1
        work = jnp.where(row == k, new0, jnp.where(row == k + 1, new1, body))
    inv_out, inv_in = work[:, 0:64], work[:, 64:128]
    zero = jnp.zeros((64, 64), F32)
    twice = jnp.concatenate(
        [jnp.concatenate([inv_in, zero], axis=1), jnp.concatenate([zero, inv_in], axis=1)], axis=0
    )
    pairs = []
    for grams in (mine, theirs):
        for d in range(0, count, 2):
            pairs.append(jnp.concatenate([grams[d, 0:64, 64:128], grams[d + 1, 0:64, 64:128]], axis=1))
    half = split_dot(jnp.concatenate(pairs, axis=0), twice)
    half = jnp.concatenate([half[64 * p : 64 * p + 64, :] for p in range(len(pairs))], axis=1)
    white = split_dot(inv_out, half)
    core = place_ref[3]
    for at in range(2 * count):
        d = at % count
        owner = core if at < count else 1 - core
        seq = (d % NY * NC + owner) * NX + d // NY
        out[seq] = white[:, 64 * at : 64 * at + 64].astype(BF16)


def full(shape, dtype=F32):
    return jax.ShapeDtypeStruct(shape, dtype)


VMEM = pl.BlockSpec(memory_space=pltpu.VMEM)
SMEM = pl.BlockSpec(memory_space=pltpu.SMEM)
ANY = pl.BlockSpec(memory_space=pl.ANY)
ZAXIS = ("zh", "zl")


def per_device(hidden, head_weight, in_proj, out_proj, targets, lengths, grad_store):
    token_count, _ = hidden.shape
    x = lax.axis_index("x")
    z = lax.axis_index("zh") * ZL + lax.axis_index("zl")
    core = lax.axis_index("c")
    rows = lax.axis_index("y") * NC + core
    place = jnp.stack([x, z, rows * NX + x, core]).astype(jnp.int32)
    cols = head_weight.shape[1]
    head = lax.all_gather(head_weight, ("y", "c"), axis=0, tiled=True)
    picked, in_rows, out_rows = pl.pallas_call(
        prepare_kernel,
        out_shape=(full((token_count, 64)), full(in_proj.shape, BF16), full(out_proj.shape, BF16)),
        in_specs=[SMEM, VMEM, VMEM, VMEM],
        out_specs=(VMEM, VMEM, VMEM),
        name="prepare",
    )(place, in_proj, out_proj, targets[:, None])
    strided = spread(hidden.T, "zh", ZH)
    strided, picked, in_rows, out_rows = lax.optimization_barrier((strided, picked, in_rows, out_rows))
    size = NX * ZH * HALF
    a_own = spread(strided[:, :HALF, :].reshape(ZH * HALF, token_count), "zl", ZL)
    a_own = a_own.reshape(size, token_count).T
    b_part = strided[:, HALF:, :].reshape(ZH * HALF, token_count).T
    b_parts = [b_part] + [shift(b_part, "x", -s, NX) for s in STEPS[1:]]
    b_own = jnp.concatenate(b_parts, axis=1)
    b_back, b_next = shift(b_own, ZAXIS, 1, NZ), shift(b_own, ZAXIS, -1, NZ)
    a_back, a_next = shift(a_own, "x", 1, NX), shift(a_own, "x", -1, NX)
    b_far, a_far = shift(b_back, ZAXIS, 1, NZ), shift(a_back, "x", 1, NX)
    chunks = [a_own, a_back, a_next, a_far, b_own, b_back, b_next, b_far]
    head = head.reshape(NX, ZH, ZL, 2, HALF, cols)
    in_rows = in_rows.reshape(NX, ZH, ZL, 2, HALF, 64)

    def buffers(count):
        return [
            pltpu.VMEM((count, token_count, size), BF16),
            pltpu.VMEM((count, NX, ZH, HALF, cols), BF16),
            pltpu.VMEM((count, NX, ZH, HALF, 64), BF16),
            pltpu.SemaphoreType.DMA((count, 1 + 2 * ZL)),
            pltpu.VMEM((token_count, cols), F32),
        ]

    acc, proj = pl.pallas_call(
        first_kernel,
        out_shape=(full((token_count, cols)), full((TILE, 64))),
        in_specs=[SMEM] + [ANY] * (len(EARLY) + 2),
        out_specs=(ANY, VMEM),
        scratch_shapes=buffers(len(EARLY)) + [pltpu.SemaphoreType.DMA((cols // BLOCK,))],
        name="logits_first",
    )(place, *[chunks[j] for j in EARLY], head, in_rows)
    packed, proj = pl.pallas_call(
        logits_kernel,
        out_shape=(full((NX * ZL, ROWS + 8, TILE)), full((TILE, 64))),
        in_specs=[SMEM] + [ANY] * (len(LATE) + 3) + [VMEM] * 3,
        out_specs=(VMEM, VMEM),
        scratch_shapes=buffers(len(LATE)) + [pltpu.SemaphoreType.DMA(())],
        name="logits_last",
    )(place, *[chunks[j] for j in LATE], head, in_rows, acc, proj, out_rows, picked)
    merged = pl.pallas_call(
        merge_kernel,
        out_shape=full((NZ, ROWS + 8, TILE)),
        in_specs=[SMEM, VMEM],
        out_specs=VMEM,
        scratch_shapes=[pltpu.VMEM((TILE, TILE), F32)],
        name="merge",
    )(place, exchange(packed, ("x", "zl")))
    seqs = NX * NY * NC
    gram = pl.pallas_call(
        gram_kernel,
        out_shape=full((NX * NY, 72, TILE)),
        in_specs=[SMEM, SMEM, VMEM, VMEM],
        out_specs=VMEM,
        name="gram",
    )(place, lengths, exchange(merged, ZAXIS), proj)
    mine = exchange(gram, ("x", "y"))
    theirs = lax.ppermute(mine, "c", [(0, 1), (1, 0)])
    whitened = pl.pallas_call(
        whiten_kernel,
        out_shape=full((seqs, 64, 64), BF16),
        in_specs=[SMEM, SMEM, VMEM, VMEM],
        out_specs=VMEM,
        name="whiten",
    )(place, lengths, mine, theirs)
    whitened = whitened.reshape(seqs, 64 * 64)
    return jnp.dot(whitened, grad_store.T, preferred_element_type=F32)


def solution(mesh):
    grid = Mesh(mesh.devices.reshape(NX, ZH, ZL, NY, NC), ("x", "zh", "zl", "y", "c"))
    return jax.shard_map(
        per_device,
        mesh=grid,
        in_specs=(
            P(("y", "c"), ("x", "zh", "zl")),
            P(("y", "c"), ("x", "zh", "zl")),
            P(),
            P(("x", "zh", "zl"), None),
            P(("y", "c")),
            P(),
            P(("x", "zh", "zl", "y", "c"), None),
        ),
        out_specs=P(None, ("x", "zh", "zl", "y", "c")),
        check_vma=False,
    )
```
